32 devices in a mesh: grp: 16 (over z, y, x), tp: 2 (over core).
Axes of the slice: x: 2, y: 2, z: 4, core: 2. Of those that a mesh axis runs over, the one named last changes fastest.
Arguments:
- qkv: bfloat16 [3, 16384, 1408], P(None, 'grp', 'tp'), as said below
- segments: int32 [16, 1024], P('grp'), may hold values from 0 to 255, as said below
- links: int32 [16], P('grp'), may hold values 0 or 1
- owners: int32 [16, 16, 1], P('grp'), may hold values from 0 to 15; in each aligned block of 16 rows (0 to 15, 16 to 31, ..., all dimensions but the last counted through in order) at most 2 rows name the same one
- merge_weight: bfloat16 [4, 1408, 1408], P(None, 'tp'), may hold values from -0.078125 to 0.078125
- norm_gain: float32 [1408], replicated, may hold values from 0.1 to 1.9
- norm_bias: float32 [1408], replicated, may hold values from -3 to 3
- next_weight: bfloat16 [1408, 4224], P(None, 'tp'), may hold values from -0.15625 to 0.15625
Outputs:
- next_qkv: bfloat16 [16, 512, 4224], P('grp', None, 'tp')
The draws below stay inside these ranges and needn't reach their ends.
Inputs may be any that keep to these rules, and one draw needn't show every extreme that they name: `qkv`: entries lie within -6 to 6. Within a row ids start at 0 and never fall; the 4 patches of one merged window share an id; a row has three or more segments; its first and its last segment hold at most 256 patches each, and in some row the first, in some row the last, holds exactly 256. `owners`: in each group's 16 blocks no owner appears more than 2 times, and some owner appears exactly 2 times.
All inputs are finite; a program needn't handle non-finite values. No bound on the sum of `links` on one device may be relied on, other than what follows from the above.
Results may differ from the reference program's by a relative error of at most 0.0062.
Values may be sent and summed in bfloat16 or wider, within the bound.
A program may use at most 192 MiB of HBM per device.

```python
import math
import jax
import jax.numpy as jnp
import numpy as np
from jax import lax

H = 16
DH = 88
L = 1024
WIN = 4
CAP = 2
D = 1408
NG = 16
TOKENS = 16384
RIM = 256
NBLK = 16


def draw_qkv(key, part):
    key = jax.random.fold_in(key, 17)
    key_base = jax.random.fold_in(key, 0)
    result = jax.random.truncated_normal(key_base, -4.0, 4.0, (3, TOKENS, D), jnp.float32)
    return result.astype(jnp.bfloat16)


def draw_segments(key, part):
    key = jax.random.fold_in(key, 29)
    key_first = jax.random.fold_in(key, 0)
    key_last = jax.random.fold_in(key, 1)
    key_row_a = jax.random.fold_in(key, 2)
    key_inner = jax.random.fold_in(key, 4)
    unit_count = L // WIN
    rim_units = RIM // WIN
    first_len = jax.random.randint(key_first, (NG,), 1, rim_units + 1)
    last_len = jax.random.randint(key_last, (NG,), 1, rim_units + 1)
    row_index = jnp.arange(NG)
    busy_row = jax.random.randint(key_row_a, (), 0, NG)
    first_row = (busy_row + 1) % NG
    last_row = (busy_row + 2) % NG
    first_len = jnp.where(row_index == first_row, rim_units, first_len)
    last_len = jnp.where(row_index == last_row, rim_units, last_len)
    position = jnp.arange(unit_count)[None, :]
    inner = jax.random.randint(key_inner, (NG, unit_count), 0, 32) == 0
    inner = jnp.logical_and(inner, jnp.logical_and(position > first_len[:, None], position < unit_count - last_len[:, None]))
    starts = jnp.logical_or(inner, jnp.logical_or(position == first_len[:, None], position == unit_count - last_len[:, None]))
    starts = jnp.where(row_index[:, None] == busy_row, position >= 1, starts)
    unit_ids = jnp.cumsum(starts.astype(jnp.int32), axis=1)
    return jnp.repeat(unit_ids, WIN, axis=1).astype(jnp.int32)


def plant(values, key, smallest, largest):
    dims = values.shape
    place = [jax.random.randint(jax.random.fold_in(key, axis), (), 0, dims[axis]) for axis in range(len(dims))]
    values = values.at[tuple(place)].set(smallest)
    longest = dims.index(max(dims))
    place[longest] = (place[longest] + 1) % dims[longest]
    return values.at[tuple(place)].set(largest)


def level_of(rng, extent, cuts, least, largest):
    def one(dim, blocks):
        draws = jax.random.uniform(jax.random.fold_in(jax.random.fold_in(rng, 6), dim), (blocks,), jnp.float32, least / len(cuts), largest / len(cuts))
        return jnp.repeat(jnp.exp(draws), extent[dim] // blocks).reshape((-1,) + (1,) * (len(extent) - dim - 1))

    loudness = one(*cuts[0])
    for cut in cuts[1:]:
        loudness = loudness * one(*cut)
    return loudness


def deal_out(key, own, number, rows, amount, top, limit, lean):
    sequence = jax.random.permutation(key, amount)
    crowded, usual = load_shares(amount, rows * top, limit, lean, True), load_shares(amount, rows * top, limit, lean, False)
    places = jnp.arange(amount)

    def named(tallies, offset_by):
        used = int((tallies > 0).sum())
        fixed = max(1, used // 4)
        shifted = fixed + (places - fixed + offset_by * (used - fixed)) % max(1, amount - fixed)
        return jnp.zeros((amount,), jnp.int32).at[sequence[jnp.where(places < fixed, places, shifted)]].set(jnp.asarray(tallies, jnp.int32))

    tallies = jnp.where(number % 4 == 0, named(crowded, number // 4), named(usual, number - number // 4 - 1))
    mixed = jax.random.permutation(jax.random.fold_in(own, 3), amount)
    source_of, receiver = mixed[0:amount // 2 * 2:2], mixed[1:amount // 2 * 2:2]
    margin = jnp.minimum(tallies[source_of] - 1, limit - tallies[receiver]) // 2
    margin = jnp.where((source_of == sequence[0]) | (receiver == sequence[0]) | (tallies[receiver] == 0), 0, jnp.maximum(margin, 0))
    shifted = jax.random.randint(jax.random.fold_in(own, 4), (amount // 2,), 0, 1 << 20) % (margin + 1)
    tallies = tallies.at[source_of].add(-shifted).at[receiver].add(shifted)
    labels = jnp.searchsorted(jnp.cumsum(tallies), jnp.arange(rows * top), side="right").astype(jnp.int32)
    grid = labels.reshape(top, rows).T
    grid = grid[jax.random.permutation(jax.random.fold_in(own, 1), rows)]
    offset_by = jax.random.randint(jax.random.fold_in(own, 2), (rows, 1), 0, top)
    return jnp.take_along_axis(grid, (jnp.arange(top)[None, :] + offset_by) % top, axis=1)


def load_shares(count, total, limit, lean, full):
    portions = [(1 << 20) // math.isqrt(standing ** lean) + 1 for standing in range(1, count + 1)]
    largest = limit if full else min(limit, max(-(-total // count), total * portions[0] // sum(portions)))
    least = 1 if total - largest >= count - 1 else 0
    given, spare = [largest] + [least] * (count - 1), total - largest - least * (count - 1)
    while spare > 0:
        free = [i for i in range(1, count) if given[i] < largest] or [i for i in range(1, count) if given[i] < limit]
        whole, left = sum([portions[i] for i in free]), spare
        for i in free:
            addition = min(limit - given[i], max(1, left * portions[i] // whole), spare)
            given[i] = given[i] + addition
            spare = spare - addition
    return np.array(given)


def noise(key, extent, width, bound, shards=(), held_as=jnp.bfloat16):
    loudness = level_of(key, extent, shards, -0.22, 0.18) if shards else 1.0
    values = jax.random.normal(key, extent, jnp.float32) * width * loudness
    return jnp.minimum(jnp.maximum(values, -bound), bound).astype(held_as)


def setup_inputs(seed: int = 0) -> dict:
    seeds = jax.random.split(jax.random.key(seed), 9)
    qkv = draw_qkv(jax.random.fold_in(seeds[8], 71), 0)
    segments = draw_segments(jax.random.fold_in(seeds[8], 71), 0)
    links = plant((jax.random.randint(seeds[2], (NG,), 0, 2) < 1).astype(jnp.int32), jax.random.fold_in(seeds[2], 1), 0, 1)
    owners_keys = jax.random.split(jax.random.fold_in(seeds[3], 1), NG * NBLK // NBLK)
    owners_turns = jax.random.permutation(jax.random.fold_in(seeds[3], 3), NG * NBLK // NBLK)
    owners = jax.vmap(lambda own, number: deal_out(jax.random.fold_in(seeds[3], 2), own, number, NBLK, NG, 1, CAP, 1))(owners_keys, owners_turns).reshape((NG, NBLK, 1))
    merge_weight = noise(seeds[4], (WIN, D, D), (WIN * D) ** -0.5, 0.078125, ((1, 2),))
    norm_gain = jnp.clip(1.0 + 0.18 * jax.random.normal(seeds[5], (D,), jnp.float32), 0.1, 1.9)
    norm_bias = noise(seeds[6], (D,), 0.5, 3.0, (), jnp.float32)
    next_weight = noise(seeds[7], (D, 3 * D), D ** -0.5, 0.15625, ((1, 2),))
    return dict(qkv=qkv, segments=segments, links=links, owners=owners, merge_weight=merge_weight, norm_gain=norm_gain, norm_bias=norm_bias, next_weight=next_weight)


def reference(qkv, segments, links, owners, merge_weight, norm_gain, norm_bias, next_weight):
    score_scale = 1.0 / math.sqrt(DH)
    group_total = segments.shape[0]
    row_len = segments.shape[1]
    model_width = H * DH
    first_seg = segments == segments[:, :1]
    last_seg = segments == segments[:, row_len - 1:]
    linked = jnp.logical_and(links > 0, jnp.arange(group_total) < group_total - 1)
    empty_row = jnp.zeros((1, row_len), dtype=bool)
    left_keys = jnp.concatenate([empty_row, jnp.logical_and(last_seg, linked[:, None])[:-1]], axis=0)
    right_keys = jnp.logical_and(jnp.concatenate([first_seg[1:], empty_row], axis=0), linked[:, None])
    padded = jnp.pad(qkv.reshape(3, group_total, row_len, H, DH), ((0, 0), (1, 1), (0, 0), (0, 0), (0, 0)))

    def attend(group):
        group = group.astype(jnp.int32)
        window = lax.dynamic_slice_in_dim(padded, group, 3, axis=1)
        queries = window[0, 1].astype(jnp.float32)
        all_keys = window[1].reshape(3 * row_len, H, DH).astype(jnp.float32)
        all_values = window[2].reshape(3 * row_len, H, DH).astype(jnp.float32)
        seg_ids = segments[group]
        same_seg = seg_ids[:, None] == seg_ids[None, :]
        left_ok = jnp.logical_and(first_seg[group][:, None], left_keys[group][None, :])
        right_ok = jnp.logical_and(last_seg[group][:, None], right_keys[group][None, :])
        allowed = jnp.concatenate([left_ok, same_seg, right_ok], axis=1)
        scores = jnp.einsum('qhd,khd->hqk', queries, all_keys) * score_scale
        scores = jnp.where(allowed[None], scores, -jnp.inf)
        row_max = lax.optimization_barrier(jnp.max(scores, axis=2, keepdims=True))
        exp_scores = jnp.exp(scores - row_max)
        weights = (exp_scores / lax.optimization_barrier(jnp.sum(exp_scores, axis=2, keepdims=True))).astype(jnp.bfloat16)
        attended_row = jnp.einsum('hqk,khd->qhd', weights.astype(jnp.float32), all_values)
        return attended_row.astype(jnp.bfloat16).reshape(row_len, model_width)
    attended = lax.map(attend, jnp.arange(group_total))
    merged = jnp.dot(attended.reshape(-1, WIN * model_width), merge_weight.reshape(WIN * model_width, model_width), preferred_element_type=jnp.float32)
    feature_mean = lax.optimization_barrier(jnp.mean(merged, axis=1, keepdims=True))
    variance = lax.optimization_barrier(jnp.mean(merged * merged, axis=1, keepdims=True)) - feature_mean * feature_mean
    normed = ((merged - feature_mean) * lax.rsqrt(variance + 1e-05) * norm_gain + norm_bias).astype(jnp.bfloat16)
    owner_ids = owners[:, :, 0].astype(jnp.int32)
    block_total = owner_ids.shape[1]
    block_index = jnp.arange(block_total)
    earlier = block_index[:, None] > block_index[None, :]
    slot_rank = lax.optimization_barrier(jnp.sum(jnp.logical_and(owner_ids[:, :, None] == owner_ids[:, None, :], earlier[None]).astype(jnp.int32), axis=2))
    block_rows = row_len // WIN // block_total
    slot_count = group_total * CAP * block_rows
    slot_base = (jnp.arange(group_total, dtype=jnp.int32)[:, None] * CAP + slot_rank) * block_rows
    slot_index = (slot_base[:, :, None] + jnp.arange(block_rows, dtype=jnp.int32)[None, None, :]).astype(jnp.int32)
    routed = jnp.zeros((group_total, slot_count, model_width), jnp.bfloat16)
    routed = routed.at[owner_ids[:, :, None], slot_index].set(normed.reshape(group_total, block_total, block_rows, model_width))
    projected = jnp.dot(routed.reshape(-1, model_width), next_weight, preferred_element_type=jnp.float32).astype(jnp.bfloat16)
    return projected.reshape(group_total, slot_count, 3 * model_width)
```

```python
import functools
import math

import jax
import jax.numpy as jnp
from jax import lax
from jax.experimental import pallas as pl
from jax.experimental.pallas import tpu as pltpu
from jax.sharding import PartitionSpec as P

DH = 88
WIN = 4
CAP = 2
TILE = 128
PACK = 16
EPS = 1e-05
NEG = -1e30
MESH = pl.DeviceIdType.MESH
SCALE2 = math.log2(math.e) / math.sqrt(DH)


def shifted(block, axis, distance):
    devices = range(lax.axis_size(axis))
    route = [(i - distance, i) for i in devices if i - distance in devices]
    return lax.ppermute(block, axis, route)


def attend_heads(width, read_query, key_parts, bias_parts, value_parts, together=4):
    pieces = []
    for base in range(0, width // DH, together):
        lows = [head * DH for head in range(base, min(base + together, width // DH))]
        scores = []
        for low in lows:
            start, stop = low // TILE * TILE, min(width, -(-(low + DH) // TILE) * TILE)
            row = start + lax.broadcasted_iota(jnp.int32, (stop - start, 1), 0)
            inside = jnp.logical_and(row >= low, row < low + DH)
            query = read_query(start, stop)
            query = jnp.where(inside, query.astype(jnp.float32), 0.0).astype(jnp.bfloat16)
            scores.append(
                [jnp.dot(keys(start, stop), query, preferred_element_type=jnp.float32) for keys in key_parts]
            )
        scores = [[part * SCALE2 + bias for part, bias in zip(parts, bias_parts)] for parts in scores]
        tops = [
            functools.reduce(jnp.maximum, [jnp.max(part, axis=0, keepdims=True) for part in parts])
            for parts in scores
        ]
        weights = [[jnp.exp2(part - top) for part in parts] for parts, top in zip(scores, tops)]
        scales = [
            1.0 / functools.reduce(jnp.add, [jnp.sum(part, axis=0, keepdims=True) for part in parts])
            for parts in weights
        ]
        weights = [
            [(part * scale).astype(jnp.bfloat16) for part in parts] for parts, scale in zip(weights, scales)
        ]
        for low, parts in zip(lows, weights):
            start, stop = low // PACK * PACK, -(-(low + DH) // PACK) * PACK
            terms = [
                jnp.dot(values(start, stop), part, preferred_element_type=jnp.float32)
                for part, values in zip(parts, value_parts)
            ]
            pieces.append(functools.reduce(jnp.add, terms)[low - start : low - start + DH])
    return jnp.concatenate(pieces, axis=0)


def attention_kernel(edge, row_len, width, sent, *refs):
    if edge:
        seg_smem, qkv_hbm, seg_row, seg_col, merge_hbm, links, prev, following, middle, out = refs[:10]
    else:
        seg_smem, qkv_hbm, seg_row, seg_col, merge_hbm, out = refs[:6]
    attended, merge_vmem, merge_sem, qkv, qkv_sem, turned_keys, turned_sides = refs[-7:]
    tiles = row_len // TILE
    edge_tiles = sent // TILE
    tokens = TILE // WIN
    fetch = pltpu.make_async_copy(merge_hbm, merge_vmem, merge_sem)
    load = pltpu.make_async_copy(qkv_hbm, qkv, qkv_sem)
    load.start()
    fetch.start()
    if edge:
        for side, source in enumerate((prev, following)):
            for at in range(0, sent, TILE):
                turned_sides[side, at : at + TILE, :] = source[0, :width, at : at + TILE].T
    load.wait()

    @pl.loop(0, tiles)
    def _(tile):
        at = pl.multiple_of(tile * TILE, TILE)
        turned_keys[pl.ds(at, TILE), :] = qkv[1, :, pl.ds(at, TILE)].T

    ordered = lax.broadcasted_iota(jnp.int32, (TILE, TILE), 0)
    ordered = (ordered % tokens) * WIN + ordered // tokens
    order = (ordered == lax.broadcasted_iota(jnp.int32, (TILE, TILE), 1)).astype(jnp.float32)
    order = order.astype(jnp.bfloat16)

    def one(tile, out_row, neighbour):
        first = seg_smem[0, tile * TILE]
        last = seg_smem[0, tile * TILE + TILE - 1]
        begin, stop = jnp.int32(0), jnp.int32(0)
        for other in range(tiles):
            begin += (seg_smem[0, other * TILE + TILE - 1] < first).astype(jnp.int32)
            stop += (seg_smem[0, other * TILE] <= last).astype(jnp.int32)
        needed = stop - begin
        query_at = pl.multiple_of(tile * TILE, TILE)
        query_ids = seg_row[pl.ds(tile, 1), :]

        def run(count):
            key_at = pl.multiple_of(jnp.minimum(begin, tiles - count) * TILE, TILE)
            key_ids = seg_col[pl.ds(key_at, count * TILE), :]
            bias_parts = [jnp.where(key_ids == query_ids, 0.0, NEG)]
            key_parts = [lambda a, b: turned_keys[pl.ds(key_at, count * TILE), a:b]]
            value_parts = [lambda a, b: qkv[2, a:b, pl.ds(key_at, count * TILE)]]
            if neighbour is not None:
                side, source, segment, open_link = neighbour
                marks = jnp.transpose(source[0, width : width + PACK, :].astype(jnp.float32))[:, :1]
                wanted = jnp.logical_and(query_ids == segment, open_link).astype(jnp.float32)
                bias_parts.append(jnp.where(marks * wanted > 0.5, 0.0, NEG))
                key_parts.append(lambda a, b: turned_sides[side, :, a:b])
                value_parts.append(lambda a, b: source[1, a:b, :])
            mixed = attend_heads(
                width,
                lambda a, b: qkv[0, a:b, pl.ds(query_at, TILE)],
                key_parts,
                bias_parts,
                value_parts,
            )
            turned = lax.dot_general(
                order,
                mixed.astype(jnp.bfloat16),
                (((1,), (1,)), ((), ())),
                preferred_element_type=jnp.float32,
            ).astype(jnp.bfloat16)
            for j in range(WIN):
                attended[j, pl.ds(out_row, tokens), :] = turned[j * tokens : (j + 1) * tokens]

        sizes = [size for size in (2, 3, 4) if size < tiles] + [tiles]
        floor = 0
        for size in sizes:
            pl.when(jnp.logical_and(needed > floor, needed <= size))(functools.partial(run, size))
            floor = size

    if edge:
        @pl.loop(0, edge_tiles)
        def _(tile):
            one(tile, pl.multiple_of(tile * tokens, tokens), (0, prev, seg_smem[0, 0], True))

        @pl.loop(0, edge_tiles)
        def _(step):
            one(
                tiles - edge_tiles + step,
                pl.multiple_of((edge_tiles + step) * tokens, tokens),
                (1, following, seg_smem[0, row_len - 1], links[0] > 0),
            )
    else:
        @pl.loop(edge_tiles, tiles - edge_tiles)
        def _(tile):
            one(tile, pl.multiple_of((tile - edge_tiles) * tokens, tokens), None)

    fetch.wait()
    merged = jnp.dot(attended[0], merge_vmem[0], preferred_element_type=jnp.float32)
    for j in range(1, WIN):
        merged += jnp.dot(attended[j], merge_vmem[j], preferred_element_type=jnp.float32)
    if edge:
        half = merged.shape[0] // 2
        out[:half, :] = merged[:half]
        out[half : half + middle.shape[0], :] = middle[...]
        out[half + middle.shape[0] :, :] = merged[half:]
    else:
        out[...] = merged


def run_attention(edge, qkv, segments, merge_weight, sent, extra):
    width, row_len = qkv.shape[1:]
    model_width = merge_weight.shape[2]
    rows = 2 * sent if edge else row_len - 2 * sent
    smem = pl.BlockSpec(memory_space=pltpu.SMEM)
    vmem = pl.BlockSpec(memory_space=pltpu.VMEM)
    operands = [
        segments,
        qkv,
        segments.reshape(row_len // TILE, TILE),
        segments.reshape(row_len, 1),
        merge_weight,
    ]
    hbm = pl.BlockSpec(memory_space=pltpu.HBM)
    specs = [smem, hbm, vmem, vmem, hbm]
    if edge:
        operands += list(extra)
        specs += [smem, vmem, vmem, vmem]
    out_rows = row_len // WIN if edge else rows // WIN
    return pl.pallas_call(
        functools.partial(attention_kernel, edge, row_len, width, sent),
        out_shape=jax.ShapeDtypeStruct((out_rows, model_width), jnp.float32),
        in_specs=specs,
        out_specs=vmem,
        scratch_shapes=[
            pltpu.VMEM((WIN, rows // WIN, width), jnp.bfloat16),
            pltpu.VMEM(merge_weight.shape, jnp.bfloat16),
            pltpu.SemaphoreType.DMA,
            pltpu.VMEM(qkv.shape, jnp.bfloat16),
            pltpu.SemaphoreType.DMA,
            pltpu.VMEM((row_len, width), jnp.bfloat16),
            pltpu.VMEM((2, sent, width), jnp.bfloat16),
        ],
        compiler_params=pltpu.CompilerParams(vmem_limit_bytes=40 << 20),
        cost_estimate=pl.CostEstimate(
            flops=rows * 512 * width * 6, bytes_accessed=qkv.size * 2, transcendentals=rows * 512 * 8
        ),
        name="edge_attention" if edge else "middle_attention",
    )(*operands)


def route_kernel(mine_ref, gain_ref, bias_ref, target_ref, routed_ref, swap_out, swap_in, packed, *sems):
    swap_sems, send_sems, recv_sems, over_sems, back_sems = sems
    group, core = lax.axis_index("grp"), lax.axis_index("tp")
    groups = lax.axis_size("grp")
    beside = 1 - core
    rows = packed.shape[0] // groups
    barrier = pltpu.get_barrier_semaphore()
    pl.semaphore_signal(barrier, inc=1, device_id=(group, beside), device_id_type=MESH)
    for step in range(1, groups):
        partner = lax.rem(group + step, groups)
        pl.semaphore_signal(barrier, inc=1, device_id=(partner, core), device_id_type=MESH)
    swap_out[...] = mine_ref[...].astype(jnp.bfloat16)
    pl.semaphore_wait(barrier, groups)
    swap = pltpu.make_async_remote_copy(
        src_ref=swap_out,
        dst_ref=swap_in,
        send_sem=swap_sems.at[0],
        recv_sem=swap_sems.at[1],
        device_id=(group, beside),
        device_id_type=MESH,
    )
    swap.start()
    place = lax.broadcasted_iota(jnp.int32, (packed.shape[0], mine_ref.shape[0]), 0)
    place = jnp.where(place == target_ref[...], 1.0, 0.0).astype(jnp.bfloat16)
    swap.wait()
    merged = mine_ref[...] + swap_in[...].astype(jnp.float32)
    model_width = merged.shape[1]
    mean = jnp.sum(merged, axis=1, keepdims=True) / model_width
    variance = jnp.sum(merged * merged, axis=1, keepdims=True) / model_width - mean * mean
    normed = (merged - mean) * lax.rsqrt(variance + EPS) * gain_ref[...] + bias_ref[...]
    packed[...] = jnp.dot(
        place, normed.astype(jnp.bfloat16), preferred_element_type=jnp.float32
    ).astype(jnp.bfloat16)

    def outgoing(step):
        partner = lax.rem(group + step, groups)
        return pltpu.make_async_remote_copy(
            src_ref=packed.at[pl.ds(pl.multiple_of(partner * rows, rows), rows), :],
            dst_ref=routed_ref.at[group, core],
            send_sem=send_sems.at[step],
            recv_sem=recv_sems.at[step],
            device_id=(partner, core),
            device_id_type=MESH,
        )

    def across(step, source):
        return pltpu.make_async_remote_copy(
            src_ref=routed_ref.at[source, core],
            dst_ref=routed_ref.at[source, core],
            send_sem=over_sems.at[step],
            recv_sem=back_sems.at[step],
            device_id=(group, beside),
            device_id_type=MESH,
        )

    for step in range(1, groups):
        outgoing(step).start()
    own = pl.multiple_of(group * rows, rows)
    routed_ref[group, core] = packed[pl.ds(own, rows), :]
    across(0, group).start()
    for step in range(1, groups):
        outgoing(step).wait_recv()
        across(step, lax.rem(group + groups - step, groups)).start()
    for step in range(groups):
        across(step, lax.rem(group + groups - step, groups)).wait()
    for step in range(1, groups):
        outgoing(step).wait_send()


def route(mine, gain, bias, target, groups):
    merged_rows, model_width = mine.shape
    rows = merged_rows // groups
    vmem = pl.BlockSpec(memory_space=pltpu.VMEM)
    return pl.pallas_call(
        route_kernel,
        out_shape=jax.ShapeDtypeStruct((groups, CAP, rows, model_width), jnp.bfloat16),
        in_specs=[vmem] * 4,
        out_specs=vmem,
        scratch_shapes=[
            pltpu.VMEM(mine.shape, jnp.bfloat16),
            pltpu.VMEM(mine.shape, jnp.bfloat16),
            pltpu.VMEM(mine.shape, jnp.bfloat16),
            pltpu.SemaphoreType.DMA((2,)),
            pltpu.SemaphoreType.DMA((groups,)),
            pltpu.SemaphoreType.DMA((groups,)),
            pltpu.SemaphoreType.DMA((groups,)),
            pltpu.SemaphoreType.DMA((groups,)),
        ],
        compiler_params=pltpu.CompilerParams(
            vmem_limit_bytes=32 << 20, collective_id=0, has_side_effects=True
        ),
        name="route",
    )(mine, gain[None], bias[None], target[None])


def project_kernel(routed_ref, weight_ref, out_ref):
    out_ref[...] = lax.dot_general(
        weight_ref[...], routed_ref[...], (((1,), (1,)), ((), ())), preferred_element_type=jnp.float32
    ).astype(jnp.bfloat16)


def project(routed, weight):
    columns, model_width = weight.shape
    slots = routed.shape[0]
    step = next(s for s in (352, 264, 176, 128, 64, 32, 16, columns) if columns % s == 0)
    return pl.pallas_call(
        project_kernel,
        grid=(columns // step,),
        out_shape=jax.ShapeDtypeStruct((columns, slots), jnp.bfloat16),
        in_specs=[
            pl.BlockSpec((slots, model_width), lambda i: (0, 0)),
            pl.BlockSpec((step, model_width), lambda i: (i, 0)),
        ],
        out_specs=pl.BlockSpec((step, slots), lambda i: (i, 0)),
        compiler_params=pltpu.CompilerParams(vmem_limit_bytes=56 << 20),
        name="project",
    )(routed, weight)


def body(qkv, segments, links, owners, merge_weight, norm_gain, norm_bias, next_weight):
    row_len = qkv.shape[1]
    model_width = norm_gain.shape[0]
    tp_size = lax.axis_size("tp")
    seg_ids = segments[0]
    linked = links[0] > 0
    sent = row_len // 4
    turned = jnp.swapaxes(qkv, 1, 2)
    last_flag = jnp.logical_and(seg_ids == seg_ids[row_len - 1], linked)[row_len - sent :]
    first_flag = (seg_ids == seg_ids[0])[:sent]

    def payload(pairs, flag):
        mark = jnp.broadcast_to(flag.astype(jnp.bfloat16)[None, None, :], (2, PACK, sent))
        return jnp.concatenate([pairs, mark], axis=1)

    prev = shifted(payload(turned[1:3, :, row_len - sent :], last_flag), "grp", 1)
    following = shifted(payload(turned[1:3, :, :sent], first_flag), "grp", -1)
    middle = run_attention(False, turned, segments, merge_weight, sent, None)
    partial_sum = run_attention(
        True, turned, segments, merge_weight, sent, (links, prev, following, middle)
    )
    merged_rows = row_len // WIN

    owner_ids = owners[0, :, 0]
    block_count = owner_ids.shape[0]
    group_count = lax.axis_size("grp")
    block_rows = merged_rows // block_count
    block_index = jnp.arange(block_count)
    earlier = block_index[:, None] > block_index[None, :]
    slot_rank = jnp.sum(
        jnp.logical_and(owner_ids[:, None] == owner_ids[None, :], earlier).astype(jnp.int32), axis=1
    )
    slots = group_count * CAP * block_rows

    if tp_size == 2 and block_count == group_count:
        mine = jnp.where(slot_rank == lax.axis_index("tp"), owner_ids, -1)
        target = mine[:, None] * block_rows + jnp.arange(block_rows)[None, :]
        target = target.reshape(merged_rows)
        routed = route(partial_sum, norm_gain, norm_bias, target, group_count)
        projected = project(routed.reshape(slots, model_width), next_weight.T)
        return projected.T[None]
    else:
        target = (owner_ids * CAP + slot_rank)[:, None] * block_rows
        target = (target + jnp.arange(block_rows)[None, :]).reshape(merged_rows)
        merged = lax.psum(partial_sum, "tp")
        mean = jnp.mean(merged, axis=1, keepdims=True)
        variance = jnp.mean(merged * merged, axis=1, keepdims=True) - mean * mean
        normed = (merged - mean) * lax.rsqrt(variance + EPS) * norm_gain + norm_bias
        normed = normed.astype(jnp.bfloat16)
        placing = (jnp.arange(slots)[:, None] == target[None, :]).astype(jnp.bfloat16)
        packed = jnp.dot(placing, normed, preferred_element_type=jnp.float32).astype(jnp.bfloat16)
        packed = packed.reshape(group_count, CAP * block_rows, model_width)
        routed = lax.all_to_all(packed, "grp", split_axis=0, concat_axis=0, tiled=True)
        routed = routed.reshape(slots, model_width)
    projected = jnp.dot(routed, next_weight, preferred_element_type=jnp.float32)
    return projected.astype(jnp.bfloat16)[None]


def solution(mesh):
    placed = (
        P(None, "grp", "tp"),
        P("grp", None),
        P("grp"),
        P("grp", None, None),
        P(None, "tp", None),
        P(),
        P(),
        P(None, "tp"),
    )
    return jax.shard_map(
        body, mesh=mesh, in_specs=placed, out_specs=P("grp", None, "tp"), check_vma=False
    )
```

```python
import functools
import math

import jax
import jax.numpy as jnp
from jax import lax
from jax.experimental import pallas as pl
from jax.experimental.pallas import tpu as pltpu
from jax.sharding import PartitionSpec as P

DH = 88
WIN = 4
CAP = 2
TILE = 128
PACK = 16
EPS = 1e-05
NEG = -1e30
MESH = pl.DeviceIdType.MESH
SPAN = 96
CODE = 640.0
SCALE2 = math.log2(math.e) / math.sqrt(DH)


def shifted(block, axis, distance):
    devices = range(lax.axis_size(axis))
    route = [(i - distance, i) for i in devices if i - distance in devices]
    return lax.ppermute(block, axis, route)


def attend_heads(width, read_query, key_parts, bias_parts, value_parts, together=4):
    pieces = []
    for base in range(0, width // DH, together):
        lows = [head * DH for head in range(base, min(base + together, width // DH))]
        scores = []
        for low in lows:
            start, stop = low // TILE * TILE, min(width, -(-(low + DH) // TILE) * TILE)
            row = start + lax.broadcasted_iota(jnp.int32, (stop - start, 1), 0)
            inside = jnp.logical_and(row >= low, row < low + DH)
            query = read_query(start, stop)
            query = jnp.where(inside, query.astype(jnp.float32), 0.0).astype(jnp.bfloat16)
            scores.append(
                [jnp.dot(keys(start, stop), query, preferred_element_type=jnp.float32) for keys in key_parts]
            )
        scores = [[part * SCALE2 + bias for part, bias in zip(parts, bias_parts)] for parts in scores]
        tops = [
            functools.reduce(jnp.maximum, [jnp.max(part, axis=0, keepdims=True) for part in parts])
            for parts in scores
        ]
        weights = [[jnp.exp2(part - top) for part in parts] for parts, top in zip(scores, tops)]
        scales = [
            1.0 / functools.reduce(jnp.add, [jnp.sum(part, axis=0, keepdims=True) for part in parts])
            for parts in weights
        ]
        weights = [
            [(part * scale).astype(jnp.bfloat16) for part in parts] for parts, scale in zip(weights, scales)
        ]
        for low, parts in zip(lows, weights):
            start, stop = low // PACK * PACK, -(-(low + DH) // PACK) * PACK
            terms = [
                jnp.dot(values(start, stop), part, preferred_element_type=jnp.float32)
                for part, values in zip(parts, value_parts)
            ]
            pieces.append(functools.reduce(jnp.add, terms)[low - start : low - start + DH])
    return jnp.concatenate(pieces, axis=0)


def attention_kernel(edge, row_len, width, sent, *refs):
    if edge:
        seg_smem, qkv_hbm, seg_row, seg_col, merge_hbm, links, prev, following, middle, out = refs[:10]
    else:
        seg_smem, qkv_hbm, seg_row, seg_col, merge_hbm, out = refs[:6]
    attended, merge_vmem, merge_sem, qkv, qkv_sem, turned_keys, turned_sides = refs[-7:]
    tiles = row_len // TILE
    edge_tiles = sent // TILE
    tokens = TILE // WIN
    fetch = pltpu.make_async_copy(merge_hbm, merge_vmem, merge_sem)
    load = pltpu.make_async_copy(qkv_hbm, qkv, qkv_sem)
    load.start()
    fetch.start()
    if edge:
        for side, source in enumerate((prev, following)):
            for at in range(0, sent, TILE):
                turned_sides[side, at : at + TILE, :] = source[0, :width, at : at + TILE].T
    load.wait()

    @pl.loop(0, tiles)
    def _(tile):
        at = pl.multiple_of(tile * TILE, TILE)
        turned_keys[pl.ds(at, TILE), :] = qkv[1, :, pl.ds(at, TILE)].T

    ordered = lax.broadcasted_iota(jnp.int32, (TILE, TILE), 0)
    ordered = (ordered % tokens) * WIN + ordered // tokens
    order = (ordered == lax.broadcasted_iota(jnp.int32, (TILE, TILE), 1)).astype(jnp.float32)
    order = order.astype(jnp.bfloat16)

    def one(tile, out_row, neighbour):
        first = seg_smem[0, tile * TILE]
        last = seg_smem[0, tile * TILE + TILE - 1]
        begin, stop = jnp.int32(0), jnp.int32(0)
        for other in range(tiles):
            begin += (seg_smem[0, other * TILE + TILE - 1] < first).astype(jnp.int32)
            stop += (seg_smem[0, other * TILE] <= last).astype(jnp.int32)
        needed = stop - begin
        query_at = pl.multiple_of(tile * TILE, TILE)
        query_ids = seg_row[pl.ds(tile, 1), :]

        def run(count):
            key_at = pl.multiple_of(jnp.minimum(begin, tiles - count) * TILE, TILE)
            key_ids = seg_col[pl.ds(key_at, count * TILE), :]
            bias_parts = [jnp.where(key_ids == query_ids, 0.0, NEG)]
            key_parts = [lambda a, b: turned_keys[pl.ds(key_at, count * TILE), a:b]]
            value_parts = [lambda a, b: qkv[2, a:b, pl.ds(key_at, count * TILE)]]
            if neighbour is not None:
                side, source, segment, open_link = neighbour
                marks = jnp.transpose(source[0, width : width + PACK, :].astype(jnp.float32))[:, :1]
                wanted = jnp.logical_and(query_ids == segment, open_link).astype(jnp.float32)
                bias_parts.append(jnp.where(marks * wanted > 0.5, 0.0, NEG))
                key_parts.append(lambda a, b: turned_sides[side, :, a:b])
                value_parts.append(lambda a, b: source[1, a:b, :])
            mixed = attend_heads(
                width,
                lambda a, b: qkv[0, a:b, pl.ds(query_at, TILE)],
                key_parts,
                bias_parts,
                value_parts,
            )
            turned = lax.dot_general(
                order,
                mixed.astype(jnp.bfloat16),
                (((1,), (1,)), ((), ())),
                preferred_element_type=jnp.float32,
            ).astype(jnp.bfloat16)
            for j in range(WIN):
                attended[j, pl.ds(out_row, tokens), :] = turned[j * tokens : (j + 1) * tokens]

        sizes = [size for size in (2, 3, 4) if size < tiles] + [tiles]
        floor = 0
        for size in sizes:
            pl.when(jnp.logical_and(needed > floor, needed <= size))(functools.partial(run, size))
            floor = size

    if edge:
        @pl.loop(0, edge_tiles)
        def _(tile):
            one(tile, pl.multiple_of(tile * tokens, tokens), (0, prev, seg_smem[0, 0], True))

        @pl.loop(0, edge_tiles)
        def _(step):
            one(
                tiles - edge_tiles + step,
                pl.multiple_of((edge_tiles + step) * tokens, tokens),
                (1, following, seg_smem[0, row_len - 1], links[0] > 0),
            )
    else:
        @pl.loop(edge_tiles, tiles - edge_tiles)
        def _(tile):
            one(tile, pl.multiple_of((tile - edge_tiles) * tokens, tokens), None)

    fetch.wait()
    merged = jnp.dot(attended[0], merge_vmem[0], preferred_element_type=jnp.float32)
    for j in range(1, WIN):
        merged += jnp.dot(attended[j], merge_vmem[j], preferred_element_type=jnp.float32)
    if edge:
        half = merged.shape[0] // 2
        out[:half, :] = merged[:half]
        out[half : half + middle.shape[0], :] = middle[...]
        out[half + middle.shape[0] :, :] = merged[half:]
    else:
        out[...] = merged


def run_attention(edge, qkv, segments, merge_weight, sent, extra):
    width, row_len = qkv.shape[1:]
    model_width = merge_weight.shape[2]
    rows = 2 * sent if edge else row_len - 2 * sent
    smem = pl.BlockSpec(memory_space=pltpu.SMEM)
    vmem = pl.BlockSpec(memory_space=pltpu.VMEM)
    operands = [
        segments,
        qkv,
        segments.reshape(row_len // TILE, TILE),
        segments.reshape(row_len, 1),
        merge_weight,
    ]
    hbm = pl.BlockSpec(memory_space=pltpu.HBM)
    specs = [smem, hbm, vmem, vmem, hbm]
    if edge:
        operands += list(extra)
        specs += [smem, vmem, vmem, vmem]
    out_rows = row_len // WIN if edge else rows // WIN
    return pl.pallas_call(
        functools.partial(attention_kernel, edge, row_len, width, sent),
        out_shape=jax.ShapeDtypeStruct((out_rows, model_width), jnp.float32),
        in_specs=specs,
        out_specs=vmem,
        scratch_shapes=[
            pltpu.VMEM((WIN, rows // WIN, width), jnp.bfloat16),
            pltpu.VMEM(merge_weight.shape, jnp.bfloat16),
            pltpu.SemaphoreType.DMA,
            pltpu.VMEM(qkv.shape, jnp.bfloat16),
            pltpu.SemaphoreType.DMA,
            pltpu.VMEM((row_len, width), jnp.bfloat16),
            pltpu.VMEM((2, sent, width), jnp.bfloat16),
        ],
        compiler_params=pltpu.CompilerParams(vmem_limit_bytes=40 << 20),
        cost_estimate=pl.CostEstimate(
            flops=rows * 512 * width * 6, bytes_accessed=qkv.size * 2, transcendentals=rows * 512 * 8
        ),
        name="edge_attention" if edge else "middle_attention",
    )(*operands)


def spread_query(query, odd, code):
    row = lax.broadcasted_iota(jnp.int32, query.shape, 0)
    inside = row >= SPAN - DH if odd else row < DH
    scaled = jnp.where(inside, query.astype(jnp.float32) * SCALE2, 0.0)
    high = scaled.astype(jnp.bfloat16)
    low = (scaled - high.astype(jnp.float32)).astype(jnp.bfloat16)
    columns = query.shape[1]
    return jnp.concatenate(
        [high, code, jnp.zeros((TILE - SPAN - PACK, columns), jnp.bfloat16)]
        + [low, jnp.zeros((TILE - SPAN, columns), jnp.bfloat16)],
        axis=0,
    )


def soft_heads(heads, read_query, code, read_keys, read_values, together=4):
    pieces, tops = [], []
    for base in range(0, heads, together):
        group = range(base, min(base + together, heads))
        scores = []
        for head in group:
            start = head * DH // PACK * PACK
            spread = spread_query(read_query(start, start + SPAN), head % 2 == 1, code)
            scores.append(jnp.dot(read_keys(head), spread, preferred_element_type=jnp.float32))
        maxima = [jnp.max(score, axis=0, keepdims=True) for score in scores]
        weights = [jnp.exp2(score - top).astype(jnp.bfloat16) for score, top in zip(scores, maxima)]
        for head, top, weight in zip(group, maxima, weights):
            mixed = jnp.dot(read_values(head), weight, preferred_element_type=jnp.float32)
            if head % 2 == 1:
                total, mixed = mixed[:1], mixed[SPAN - DH :]
            else:
                total, mixed = mixed[DH : DH + 1], mixed[:DH]
            pieces.append(mixed * (1.0 / total))
            tops.append(top + jnp.log2(total))
    return jnp.concatenate(pieces, axis=0), jnp.concatenate(tops, axis=0)


def encoder_kernel(
    qkv_hbm,
    merge_hbm,
    seg_ref,
    link_ref,
    owner_ref,
    gain_ref,
    bias_ref,
    routed_ref,
    qkv,
    merge,
    spread_keys,
    spread_values,
    local_mixed,
    local_stats,
    far_mixed,
    far_stats,
    query_in,
    stats_out,
    stats_in,
    back_out,
    back_in,
    attended_mid,
    attended_far,
    attended_edge,
    far_part,
    far_low,
    far_swap,
    part_out,
    part_in,
    mid_part,
    mid_swap,
    edge_part,
    edge_low,
    edge_swap,
    normed,
    packed,
    load_sems,
    merge_sems,
    next_send,
    next_recv,
    swap_send,
    swap_recv,
    send_sems,
    recv_sems,
    over_sems,
    back_sems,
):
    group, core = lax.axis_index("grp"), lax.axis_index("tp")
    groups = lax.axis_size("grp")
    beside = 1 - core
    width, row_len = qkv.shape[1:]
    heads = width // DH
    sent = query_in.shape[2]
    parts = row_len // sent
    tokens = sent // WIN
    rows = packed.shape[0] // groups
    model_width = merge.shape[2]
    has_prev, has_next = group > 0, group < groups - 1

    barrier = pltpu.get_barrier_semaphore()
    pl.semaphore_signal(barrier, inc=1, device_id=(group, beside), device_id_type=MESH)
    for step in range(1, groups):
        partner = lax.rem(group + step, groups)
        pl.semaphore_signal(barrier, inc=1, device_id=(partner, core), device_id_type=MESH)
    loads = [pltpu.make_async_copy(qkv_hbm.at[i], qkv.at[i], load_sems.at[i]) for i in range(3)]
    loads[1].start()
    loads[0].start()
    loads[2].start()
    fetches = [
        pltpu.make_async_copy(merge_hbm.at[j], merge.at[j], merge_sems.at[j]) for j in range(WIN)
    ]
    for fetch in fetches:
        fetch.start()

    def along(kind, side, source, target):
        partner = lax.rem(group + groups - 1, groups) if side == 0 else lax.rem(group + 1, groups)
        return pltpu.make_async_remote_copy(
            src_ref=source,
            dst_ref=target.at[1 - side],
            send_sem=next_send.at[kind, side],
            recv_sem=next_recv.at[kind, 1 - side],
            device_id=(partner, core),
            device_id_type=MESH,
        )

    def across(kind, source, target):
        return pltpu.make_async_remote_copy(
            src_ref=source,
            dst_ref=target,
            send_sem=swap_send.at[kind],
            recv_sem=swap_recv.at[kind],
            device_id=(group, beside),
            device_id_type=MESH,
        )

    query_moves = [
        along(0, side, qkv_hbm.at[0, :, pl.ds(side * (row_len - sent), sent)], query_in)
        for side in range(2)
    ]
    stats_moves = [along(1, side, stats_out.at[side], stats_in) for side in range(2)]
    back_moves = [along(2, side, back_out.at[side], back_in) for side in range(2)]
    part_moves = [along(3, side, part_out.at[side], part_in) for side in range(2)]
    exists = [has_prev, has_next]

    def begin(moves, side):
        pl.when(exists[side])(lambda: moves[side].start())

    def landed(moves, slot):
        pl.when(exists[slot])(lambda: moves[1 - slot].wait_recv())

    def left(moves, side):
        pl.when(exists[side])(lambda: moves[side].wait_send())

    for slot in range(2):
        @pl.when(jnp.logical_not(exists[slot]))
        def _():
            query_in[slot] = jnp.zeros(query_in.shape[1:], query_in.dtype)
            stats_in[slot] = jnp.full(stats_in.shape[1:], -NEG, jnp.float32)
            back_in[slot] = jnp.full(back_in.shape[1:], NEG, jnp.float32)
            part_in[slot] = jnp.zeros(part_in.shape[1:], part_in.dtype)

    seg = seg_ref[...]
    bit = jnp.left_shift(1, lax.broadcasted_iota(jnp.int32, (PACK, 1), 0))
    real = lax.broadcasted_iota(jnp.int32, (PACK, 1), 0) < 8

    def code_of(ids, size):
        sign = jnp.where(jnp.bitwise_and(ids, bit) != 0, size, -size)
        return jnp.where(real, sign, 0.0).astype(jnp.bfloat16)

    pl.semaphore_wait(barrier, groups)
    begin(query_moves, 0)
    begin(query_moves, 1)

    key_code = code_of(seg, 1.0)
    key_fill = jnp.zeros((TILE - SPAN - PACK, row_len), jnp.bfloat16)
    loads[1].wait()
    for head in range(heads):
        start = head * DH // PACK * PACK
        block = jnp.concatenate([qkv[1, start : start + SPAN, :], key_code, key_fill], axis=0).T
        spread_keys[head, :, :TILE] = block
        spread_keys[head, :, TILE:] = block
    loads[2].wait()
    span_row = lax.broadcasted_iota(jnp.int32, (SPAN, 1), 0)
    for head in range(heads):
        start = head * DH // PACK * PACK
        spare = span_row < SPAN - DH if head % 2 == 1 else span_row >= DH
        value = qkv[2, start : start + SPAN, :].astype(jnp.float32)
        spread_values[head] = jnp.where(spare, 1.0, value).astype(jnp.bfloat16)
    loads[0].wait()

    @pl.loop(0, parts)
    def _(part):
        at = pl.multiple_of(part * sent, sent)
        mixed, stats = soft_heads(
            heads,
            lambda a, b: qkv[0, a:b, pl.ds(at, sent)],
            code_of(seg_ref[:, pl.ds(at, sent)], CODE),
            lambda head: spread_keys[head],
            lambda head: spread_values[head],
        )
        local_mixed[part] = mixed
        local_stats[part] = stats

    first_id, last_id = seg[:, :1], seg[:, row_len - 1 :]
    link_open = jnp.logical_and(link_ref[...] > 0, has_next)
    in_first = seg[:, :sent] == first_id
    in_last = jnp.logical_and(seg[:, row_len - sent :] == last_id, link_open)
    inside = [in_first, in_last]
    stats_out[0] = jnp.where(in_first, local_stats[0], -NEG)
    stats_out[1] = jnp.where(in_last, local_stats[parts - 1], -NEG)
    begin(stats_moves, 0)
    begin(stats_moves, 1)

    ordered = lax.broadcasted_iota(jnp.int32, (sent, sent), 0)
    ordered = (ordered % tokens) * WIN + ordered // tokens
    order = (ordered == lax.broadcasted_iota(jnp.int32, (sent, sent), 1)).astype(jnp.float32)
    order = order.astype(jnp.bfloat16)

    def turn(mixed, target, at):
        turned = lax.dot_general(
            order,
            mixed.astype(jnp.bfloat16),
            (((1,), (1,)), ((), ())),
            preferred_element_type=jnp.float32,
        ).astype(jnp.bfloat16)
        for j in range(WIN):
            target[j, at : at + tokens, :] = turned[j * tokens : (j + 1) * tokens]

    def merge_rows(attended):
        merged = jnp.dot(attended[0], merge[0], preferred_element_type=jnp.float32)
        for j in range(1, WIN):
            merged += jnp.dot(attended[j], merge[j], preferred_element_type=jnp.float32)
        return merged

    def scaled_heads(mixed, scale):
        return jnp.concatenate(
            [mixed[h * DH : (h + 1) * DH] * scale[h : h + 1] for h in range(heads)], axis=0
        )

    for part in range(1, parts - 1):
        turn(local_mixed[part], attended_mid, (part - 1) * tokens)
    for fetch in fetches:
        fetch.wait()
    mid_part[...] = merge_rows(attended_mid)
    mid_move = across(0, mid_part, mid_swap)
    mid_move.start()

    for side in range(2):
        keys_at = side * (row_len - sent)
        code = code_of(first_id if side == 0 else last_id, CODE)
        landed(query_moves, side)
        mixed, stats = soft_heads(
            heads,
            lambda a, b: query_in[side, a:b, :],
            jnp.broadcast_to(code.astype(jnp.float32), (PACK, sent)).astype(jnp.bfloat16),
            lambda head: spread_keys[head, keys_at : keys_at + sent, :],
            lambda head: spread_values[head, :, keys_at : keys_at + sent],
        )
        if side == 1:
            stats = jnp.where(link_open, stats, NEG)
        far_mixed[side] = mixed
        far_stats[side] = stats
        back_out[side] = stats
        begin(back_moves, side)
    for side in range(2):
        landed(stats_moves, side)
        share = 1.0 / (1.0 + jnp.exp2(stats_in[side] - far_stats[side]))
        turn(scaled_heads(far_mixed[side], share), attended_far, side * tokens)
    far_merged = merge_rows(attended_far)
    half = tokens // 2
    for side in range(2):
        for part in range(2):
            piece = far_merged[side * tokens + part * half : side * tokens + (part + 1) * half]
            far_part[part, side] = piece
            far_low[part, side] = piece.astype(jnp.bfloat16)
    far_move = across(1, far_low.at[beside], far_swap)
    far_move.start()
    far_move.wait_recv()
    for side in range(2):
        part_out[side] = (far_part[core, side] + far_swap[side].astype(jnp.float32)).astype(jnp.bfloat16)
        begin(part_moves, side)

    for side in range(2):
        landed(back_moves, side)
        back = jnp.where(inside[side], back_in[side], NEG)
        place_at = side * (parts - 1)
        share = 1.0 / (1.0 + jnp.exp2(back - local_stats[place_at]))
        turn(scaled_heads(local_mixed[place_at], share), attended_edge, side * tokens)
    edge_merged = merge_rows(attended_edge)
    for side in range(2):
        for part in range(2):
            at = side * tokens + part * half
            edge_part[part, side] = edge_merged[at : at + half]

    def norm(merged):
        mean = jnp.sum(merged, axis=1, keepdims=True) / model_width
        variance = jnp.sum(merged * merged, axis=1, keepdims=True) / model_width - mean * mean
        value = (merged - mean) * lax.rsqrt(variance + EPS) * gain_ref[...] + bias_ref[...]
        return value.astype(jnp.bfloat16)

    mid_move.wait_recv()
    normed[tokens : (parts - 1) * tokens, :] = norm(mid_part[...] + mid_swap[...])

    blocks, merged_rows = owner_ref.shape[1], packed.shape[0]
    same = lax.broadcasted_iota(jnp.int32, (blocks, blocks), 0)
    same = same == lax.broadcasted_iota(jnp.int32, (blocks, blocks), 1)
    owner_col = jnp.sum(jnp.where(same, owner_ref[...], 0), axis=1, keepdims=True)
    block_row = lax.broadcasted_iota(jnp.int32, (blocks, merged_rows), 0)
    block_of = lax.broadcasted_iota(jnp.int32, (blocks, merged_rows), 1) // rows
    owner_of = jnp.sum(jnp.where(block_row == block_of, owner_col, 0), axis=0, keepdims=True)
    earlier = jnp.logical_and(owner_col == owner_of, block_row < block_of)
    rank = jnp.sum(jnp.where(earlier, 1, 0), axis=0, keepdims=True)
    token = lax.broadcasted_iota(jnp.int32, (1, merged_rows), 1)
    target = jnp.where(rank == core, owner_of * rows + token % rows, -1)
    place = lax.broadcasted_iota(jnp.int32, (merged_rows, merged_rows), 0)
    place = jnp.where(place == target, 1.0, 0.0).astype(jnp.bfloat16)

    for side in range(2):
        landed(part_moves, side)
        edge_part[core, side] = edge_part[core, side] + part_in[side].astype(jnp.float32)
    edge_low[...] = edge_part[...].astype(jnp.bfloat16)
    edge_move = across(2, edge_low, edge_swap)
    edge_move.start()
    edge_move.wait_recv()
    for side in range(2):
        for part in range(2):
            at = side * (parts - 1) * tokens + part * half
            value = edge_part[part, side] + edge_swap[part, side].astype(jnp.float32)
            normed[at : at + half, :] = norm(value)
    packed[...] = jnp.dot(place, normed[...], preferred_element_type=jnp.float32).astype(jnp.bfloat16)

    def outgoing(step):
        partner = lax.rem(group + step, groups)
        return pltpu.make_async_remote_copy(
            src_ref=packed.at[pl.ds(pl.multiple_of(partner * rows, rows), rows), :],
            dst_ref=routed_ref.at[group, core],
            send_sem=send_sems.at[step],
            recv_sem=recv_sems.at[step],
            device_id=(partner, core),
            device_id_type=MESH,
        )

    def handed(step):
        source = lax.rem(group + groups - step, groups)
        return pltpu.make_async_remote_copy(
            src_ref=routed_ref.at[source, core],
            dst_ref=routed_ref.at[source, core],
            send_sem=over_sems.at[step],
            recv_sem=back_sems.at[step],
            device_id=(group, beside),
            device_id_type=MESH,
        )

    for step in range(1, groups):
        outgoing(step).start()
    own = pl.multiple_of(group * rows, rows)
    routed_ref[group, core] = packed[pl.ds(own, rows), :]
    handed(0).start()
    for step in range(1, groups):
        outgoing(step).wait_recv()
        handed(step).start()
    for side in range(2):
        for moves in (query_moves, stats_moves, back_moves, part_moves):
            left(moves, side)
    for move in (mid_move, far_move, edge_move):
        move.wait_send()
    for step in range(groups):
        handed(step).wait()
    for step in range(1, groups):
        outgoing(step).wait_send()


def encode(qkv, merge_weight, segments, links, owners, gain, bias, groups):
    width, row_len = qkv.shape[1:]
    model_width = merge_weight.shape[2]
    heads = width // DH
    parts = 4
    sent = row_len // parts
    tokens = sent // WIN
    merged_rows = row_len // WIN
    rows = merged_rows // groups
    vmem = pl.BlockSpec(memory_space=pltpu.VMEM)
    hbm = pl.BlockSpec(memory_space=pltpu.HBM)
    low, full = jnp.bfloat16, jnp.float32
    return pl.pallas_call(
        encoder_kernel,
        out_shape=jax.ShapeDtypeStruct((groups, CAP, rows, model_width), low),
        in_specs=[hbm, hbm, vmem, vmem, vmem, vmem, vmem],
        out_specs=vmem,
        scratch_shapes=[
            pltpu.VMEM(qkv.shape, low),
            pltpu.VMEM(merge_weight.shape, low),
            pltpu.VMEM((heads, row_len, 2 * TILE), low),
            pltpu.VMEM((heads, SPAN, row_len), low),
            pltpu.VMEM((parts, width, sent), full),
            pltpu.VMEM((parts, heads, sent), full),
            pltpu.VMEM((2, width, sent), full),
            pltpu.VMEM((2, heads, sent), full),
            pltpu.VMEM((2, width, sent), low),
            pltpu.VMEM((2, heads, sent), full),
            pltpu.VMEM((2, heads, sent), full),
            pltpu.VMEM((2, heads, sent), full),
            pltpu.VMEM((2, heads, sent), full),
            pltpu.VMEM((WIN, 2 * tokens, width), low),
            pltpu.VMEM((WIN, 2 * tokens, width), low),
            pltpu.VMEM((WIN, 2 * tokens, width), low),
            pltpu.VMEM((2, 2, tokens // 2, model_width), full),
            pltpu.VMEM((2, 2, tokens // 2, model_width), low),
            pltpu.VMEM((2, tokens // 2, model_width), low),
            pltpu.VMEM((2, tokens // 2, model_width), low),
            pltpu.VMEM((2, tokens // 2, model_width), low),
            pltpu.VMEM((2 * tokens, model_width), full),
            pltpu.VMEM((2 * tokens, model_width), full),
            pltpu.VMEM((2, 2, tokens // 2, model_width), full),
            pltpu.VMEM((2, 2, tokens // 2, model_width), low),
            pltpu.VMEM((2, 2, tokens // 2, model_width), low),
            pltpu.VMEM((merged_rows, model_width), low),
            pltpu.VMEM((merged_rows, model_width), low),
            pltpu.SemaphoreType.DMA((3,)),
            pltpu.SemaphoreType.DMA((WIN,)),
            pltpu.SemaphoreType.DMA((4, 2)),
            pltpu.SemaphoreType.DMA((4, 2)),
            pltpu.SemaphoreType.DMA((3,)),
            pltpu.SemaphoreType.DMA((3,)),
            pltpu.SemaphoreType.DMA((groups,)),
            pltpu.SemaphoreType.DMA((groups,)),
            pltpu.SemaphoreType.DMA((groups,)),
            pltpu.SemaphoreType.DMA((groups,)),
        ],
        compiler_params=pltpu.CompilerParams(
            vmem_limit_bytes=56 << 20, collective_id=0, has_side_effects=True
        ),
        name="encode",
    )(qkv, merge_weight, segments, links.reshape(1, 1), owners, gain[None], bias[None])


def project_kernel(routed_ref, weight_ref, out_ref):
    out_ref[...] = lax.dot_general(
        weight_ref[...], routed_ref[...], (((1,), (1,)), ((), ())), preferred_element_type=jnp.float32
    ).astype(jnp.bfloat16)


def project(routed, weight):
    columns, model_width = weight.shape
    slots = routed.shape[0]
    step = next(s for s in (352, 264, 176, 128, 64, 32, 16, columns) if columns % s == 0)
    return pl.pallas_call(
        project_kernel,
        grid=(columns // step,),
        out_shape=jax.ShapeDtypeStruct((columns, slots), jnp.bfloat16),
        in_specs=[
            pl.BlockSpec((slots, model_width), lambda i: (0, 0)),
            pl.BlockSpec((step, model_width), lambda i: (i, 0)),
        ],
        out_specs=pl.BlockSpec((step, slots), lambda i: (i, 0)),
        compiler_params=pltpu.CompilerParams(vmem_limit_bytes=56 << 20),
        name="project",
    )(routed, weight)


def body(qkv, segments, links, owners, merge_weight, norm_gain, norm_bias, next_weight):
    row_len = qkv.shape[1]
    model_width = norm_gain.shape[0]
    tp_size = lax.axis_size("tp")
    turned = jnp.swapaxes(qkv, 1, 2)
    group_count = lax.axis_size("grp")
    owner_ids = owners[0, :, 0]
    block_count = owner_ids.shape[0]
    if tp_size == 2 and block_count == group_count:
        routed = encode(
            turned, merge_weight, segments, links, owner_ids[None], norm_gain, norm_bias, group_count
        )
        routed = routed.reshape(-1, model_width)
        return project(routed, next_weight.T).T[None]
    seg_ids = segments[0]
    linked = links[0] > 0
    sent = row_len // 4
    last_flag = jnp.logical_and(seg_ids == seg_ids[row_len - 1], linked)[row_len - sent :]
    first_flag = (seg_ids == seg_ids[0])[:sent]

    def payload(pairs, flag):
        mark = jnp.broadcast_to(flag.astype(jnp.bfloat16)[None, None, :], (2, PACK, sent))
        return jnp.concatenate([pairs, mark], axis=1)

    prev = shifted(payload(turned[1:3, :, row_len - sent :], last_flag), "grp", 1)
    following = shifted(payload(turned[1:3, :, :sent], first_flag), "grp", -1)
    middle = run_attention(False, turned, segments, merge_weight, sent, None)
    partial_sum = run_attention(
        True, turned, segments, merge_weight, sent, (links, prev, following, middle)
    )
    merged_rows = row_len // WIN

    block_rows = merged_rows // block_count
    block_index = jnp.arange(block_count)
    earlier = block_index[:, None] > block_index[None, :]
    slot_rank = jnp.sum(
        jnp.logical_and(owner_ids[:, None] == owner_ids[None, :], earlier).astype(jnp.int32), axis=1
    )
    slots = group_count * CAP * block_rows

    target = (owner_ids * CAP + slot_rank)[:, None] * block_rows
    target = (target + jnp.arange(block_rows)[None, :]).reshape(merged_rows)
    merged = lax.psum(partial_sum, "tp")
    mean = jnp.mean(merged, axis=1, keepdims=True)
    variance = jnp.mean(merged * merged, axis=1, keepdims=True) - mean * mean
    normed = (merged - mean) * lax.rsqrt(variance + EPS) * norm_gain + norm_bias
    normed = normed.astype(jnp.bfloat16)
    placing = (jnp.arange(slots)[:, None] == target[None, :]).astype(jnp.bfloat16)
    packed = jnp.dot(placing, normed, preferred_element_type=jnp.float32).astype(jnp.bfloat16)
    packed = packed.reshape(group_count, CAP * block_rows, model_width)
    routed = lax.all_to_all(packed, "grp", split_axis=0, concat_axis=0, tiled=True)
    routed = routed.reshape(slots, model_width)
    projected = jnp.dot(routed, next_weight, preferred_element_type=jnp.float32)
    return projected.astype(jnp.bfloat16)[None]


def solution(mesh):
    placed = (
        P(None, "grp", "tp"),
        P("grp", None),
        P("grp"),
        P("grp", None, None),
        P(None, "tp", None),
        P(),
        P(),
        P(None, "tp"),
    )
    return jax.shard_map(
        body, mesh=mesh, in_specs=placed, out_specs=P("grp", None, "tp"), check_vma=False
    )
```

```python
import functools
import math

import jax
import jax.numpy as jnp
from jax import lax
from jax.experimental import pallas as pl
from jax.experimental.pallas import tpu as pltpu
from jax.sharding import PartitionSpec as P

DH = 88
WIN = 4
CAP = 2
TILE = 128
PACK = 16
EPS = 1e-05
NEG = -1e30
MESH = pl.DeviceIdType.MESH
SPAN = 96
CODE = 640.0
SCALE2 = math.log2(math.e) / math.sqrt(DH)


def shifted(block, axis, distance):
    devices = range(lax.axis_size(axis))
    route = [(i - distance, i) for i in devices if i - distance in devices]
    return lax.ppermute(block, axis, route)


def attend_heads(width, read_query, key_parts, bias_parts, value_parts, together=4):
    pieces = []
    for base in range(0, width // DH, together):
        lows = [head * DH for head in range(base, min(base + together, width // DH))]
        scores = []
        for low in lows:
            start, stop = low // TILE * TILE, min(width, -(-(low + DH) // TILE) * TILE)
            row = start + lax.broadcasted_iota(jnp.int32, (stop - start, 1), 0)
            inside = jnp.logical_and(row >= low, row < low + DH)
            query = read_query(start, stop)
            query = jnp.where(inside, query.astype(jnp.float32), 0.0).astype(jnp.bfloat16)
            scores.append(
                [jnp.dot(keys(start, stop), query, preferred_element_type=jnp.float32) for keys in key_parts]
            )
        scores = [[part * SCALE2 + bias for part, bias in zip(parts, bias_parts)] for parts in scores]
        tops = [
            functools.reduce(jnp.maximum, [jnp.max(part, axis=0, keepdims=True) for part in parts])
            for parts in scores
        ]
        weights = [[jnp.exp2(part - top) for part in parts] for parts, top in zip(scores, tops)]
        scales = [
            1.0 / functools.reduce(jnp.add, [jnp.sum(part, axis=0, keepdims=True) for part in parts])
            for parts in weights
        ]
        weights = [
            [(part * scale).astype(jnp.bfloat16) for part in parts] for parts, scale in zip(weights, scales)
        ]
        for low, parts in zip(lows, weights):
            start, stop = low // PACK * PACK, -(-(low + DH) // PACK) * PACK
            terms = [
                jnp.dot(values(start, stop), part, preferred_element_type=jnp.float32)
                for part, values in zip(parts, value_parts)
            ]
            pieces.append(functools.reduce(jnp.add, terms)[low - start : low - start + DH])
    return jnp.concatenate(pieces, axis=0)


def attention_kernel(edge, row_len, width, sent, *refs):
    if edge:
        seg_smem, qkv_hbm, seg_row, seg_col, merge_hbm, links, prev, following, middle, out = refs[:10]
    else:
        seg_smem, qkv_hbm, seg_row, seg_col, merge_hbm, out = refs[:6]
    attended, merge_vmem, merge_sem, qkv, qkv_sem, turned_keys, turned_sides = refs[-7:]
    tiles = row_len // TILE
    edge_tiles = sent // TILE
    tokens = TILE // WIN
    fetch = pltpu.make_async_copy(merge_hbm, merge_vmem, merge_sem)
    load = pltpu.make_async_copy(qkv_hbm, qkv, qkv_sem)
    load.start()
    fetch.start()
    if edge:
        for side, source in enumerate((prev, following)):
            for at in range(0, sent, TILE):
                turned_sides[side, at : at + TILE, :] = source[0, :width, at : at + TILE].T
    load.wait()

    @pl.loop(0, tiles)
    def _(tile):
        at = pl.multiple_of(tile * TILE, TILE)
        turned_keys[pl.ds(at, TILE), :] = qkv[1, :, pl.ds(at, TILE)].T

    ordered = lax.broadcasted_iota(jnp.int32, (TILE, TILE), 0)
    ordered = (ordered % tokens) * WIN + ordered // tokens
    order = (ordered == lax.broadcasted_iota(jnp.int32, (TILE, TILE), 1)).astype(jnp.float32)
    order = order.astype(jnp.bfloat16)

    def one(tile, out_row, neighbour):
        first = seg_smem[0, tile * TILE]
        last = seg_smem[0, tile * TILE + TILE - 1]
        begin, stop = jnp.int32(0), jnp.int32(0)
        for other in range(tiles):
            begin += (seg_smem[0, other * TILE + TILE - 1] < first).astype(jnp.int32)
            stop += (seg_smem[0, other * TILE] <= last).astype(jnp.int32)
        needed = stop - begin
        query_at = pl.multiple_of(tile * TILE, TILE)
        query_ids = seg_row[pl.ds(tile, 1), :]

        def run(count):
            key_at = pl.multiple_of(jnp.minimum(begin, tiles - count) * TILE, TILE)
            key_ids = seg_col[pl.ds(key_at, count * TILE), :]
            bias_parts = [jnp.where(key_ids == query_ids, 0.0, NEG)]
            key_parts = [lambda a, b: turned_keys[pl.ds(key_at, count * TILE), a:b]]
            value_parts = [lambda a, b: qkv[2, a:b, pl.ds(key_at, count * TILE)]]
            if neighbour is not None:
                side, source, segment, open_link = neighbour
                marks = jnp.transpose(source[0, width : width + PACK, :].astype(jnp.float32))[:, :1]
                wanted = jnp.logical_and(query_ids == segment, open_link).astype(jnp.float32)
                bias_parts.append(jnp.where(marks * wanted > 0.5, 0.0, NEG))
                key_parts.append(lambda a, b: turned_sides[side, :, a:b])
                value_parts.append(lambda a, b: source[1, a:b, :])
            mixed = attend_heads(
                width,
                lambda a, b: qkv[0, a:b, pl.ds(query_at, TILE)],
                key_parts,
                bias_parts,
                value_parts,
            )
            turned = lax.dot_general(
                order,
                mixed.astype(jnp.bfloat16),
                (((1,), (1,)), ((), ())),
                preferred_element_type=jnp.float32,
            ).astype(jnp.bfloat16)
            for j in range(WIN):
                attended[j, pl.ds(out_row, tokens), :] = turned[j * tokens : (j + 1) * tokens]

        sizes = [size for size in (2, 3, 4) if size < tiles] + [tiles]
        floor = 0
        for size in sizes:
            pl.when(jnp.logical_and(needed > floor, needed <= size))(functools.partial(run, size))
            floor = size

    if edge:
        @pl.loop(0, edge_tiles)
        def _(tile):
            one(tile, pl.multiple_of(tile * tokens, tokens), (0, prev, seg_smem[0, 0], True))

        @pl.loop(0, edge_tiles)
        def _(step):
            one(
                tiles - edge_tiles + step,
                pl.multiple_of((edge_tiles + step) * tokens, tokens),
                (1, following, seg_smem[0, row_len - 1], links[0] > 0),
            )
    else:
        @pl.loop(edge_tiles, tiles - edge_tiles)
        def _(tile):
            one(tile, pl.multiple_of((tile - edge_tiles) * tokens, tokens), None)

    fetch.wait()
    merged = jnp.dot(attended[0], merge_vmem[0], preferred_element_type=jnp.float32)
    for j in range(1, WIN):
        merged += jnp.dot(attended[j], merge_vmem[j], preferred_element_type=jnp.float32)
    if edge:
        half = merged.shape[0] // 2
        out[:half, :] = merged[:half]
        out[half : half + middle.shape[0], :] = middle[...]
        out[half + middle.shape[0] :, :] = merged[half:]
    else:
        out[...] = merged


def run_attention(edge, qkv, segments, merge_weight, sent, extra):
    width, row_len = qkv.shape[1:]
    model_width = merge_weight.shape[2]
    rows = 2 * sent if edge else row_len - 2 * sent
    smem = pl.BlockSpec(memory_space=pltpu.SMEM)
    vmem = pl.BlockSpec(memory_space=pltpu.VMEM)
    operands = [
        segments,
        qkv,
        segments.reshape(row_len // TILE, TILE),
        segments.reshape(row_len, 1),
        merge_weight,
    ]
    hbm = pl.BlockSpec(memory_space=pltpu.HBM)
    specs = [smem, hbm, vmem, vmem, hbm]
    if edge:
        operands += list(extra)
        specs += [smem, vmem, vmem, vmem]
    out_rows = row_len // WIN if edge else rows // WIN
    return pl.pallas_call(
        functools.partial(attention_kernel, edge, row_len, width, sent),
        out_shape=jax.ShapeDtypeStruct((out_rows, model_width), jnp.float32),
        in_specs=specs,
        out_specs=vmem,
        scratch_shapes=[
            pltpu.VMEM((WIN, rows // WIN, width), jnp.bfloat16),
            pltpu.VMEM(merge_weight.shape, jnp.bfloat16),
            pltpu.SemaphoreType.DMA,
            pltpu.VMEM(qkv.shape, jnp.bfloat16),
            pltpu.SemaphoreType.DMA,
            pltpu.VMEM((row_len, width), jnp.bfloat16),
            pltpu.VMEM((2, sent, width), jnp.bfloat16),
        ],
        compiler_params=pltpu.CompilerParams(vmem_limit_bytes=40 << 20),
        cost_estimate=pl.CostEstimate(
            flops=rows * 512 * width * 6, bytes_accessed=qkv.size * 2, transcendentals=rows * 512 * 8
        ),
        name="edge_attention" if edge else "middle_attention",
    )(*operands)


def spread_query(query, odd, code):
    row = lax.broadcasted_iota(jnp.int32, query.shape, 0)
    inside = row >= SPAN - DH if odd else row < DH
    scaled = jnp.where(inside, query.astype(jnp.float32) * SCALE2, 0.0)
    high = scaled.astype(jnp.bfloat16)
    low = (scaled - high.astype(jnp.float32)).astype(jnp.bfloat16)
    columns = query.shape[1]
    return jnp.concatenate(
        [high, code, jnp.zeros((TILE - SPAN - PACK, columns), jnp.bfloat16)]
        + [low, jnp.zeros((TILE - SPAN, columns), jnp.bfloat16)],
        axis=0,
    )


def soft_heads(heads, read_query, code, read_keys, read_values, together=4):
    pieces, tops = [], []
    for base in range(0, heads, together):
        group = range(base, min(base + together, heads))
        scores = []
        for head in group:
            start = head * DH // PACK * PACK
            spread = spread_query(read_query(start, start + SPAN), head % 2 == 1, code)
            scores.append(jnp.dot(read_keys(head), spread, preferred_element_type=jnp.float32))
        maxima = [jnp.max(score, axis=0, keepdims=True) for score in scores]
        weights = [jnp.exp2(score - top).astype(jnp.bfloat16) for score, top in zip(scores, maxima)]
        for head, top, weight in zip(group, maxima, weights):
            mixed = jnp.dot(read_values(head), weight, preferred_element_type=jnp.float32)
            if head % 2 == 1:
                total, mixed = mixed[:1], mixed[SPAN - DH :]
            else:
                total, mixed = mixed[DH : DH + 1], mixed[:DH]
            pieces.append(mixed * (1.0 / total))
            tops.append(top + jnp.log2(total))
    return jnp.concatenate(pieces, axis=0), jnp.concatenate(tops, axis=0)


def encoder_kernel(
    qkv_hbm,
    merge_hbm,
    small_ref,
    next_hbm,
    out_ref,
    routed_ref,
    next_weight,
    routed_turned,
    qkv,
    merge,
    spread_keys,
    spread_values,
    local_mixed,
    local_stats,
    far_mixed,
    far_stats,
    query_in,
    stats_out,
    stats_in,
    back_out,
    back_in,
    attended_mid,
    attended_far,
    attended_edge,
    far_part,
    far_low,
    far_swap,
    part_out,
    part_in,
    mid_part,
    mid_swap,
    part_far,
    edge_part,
    edge_swap,
    normed,
    packed,
    load_sems,
    merge_sems,
    next_sem,
    next_send,
    next_recv,
    swap_send,
    swap_recv,
    send_sems,
    recv_sems,
    over_sems,
    back_sems,
):
    group, core = lax.axis_index("grp"), lax.axis_index("tp")
    groups = lax.axis_size("grp")
    beside = 1 - core
    width, row_len = qkv.shape[1:]
    heads = width // DH
    sent = query_in.shape[2]
    parts = row_len // sent
    tokens = sent // WIN
    rows = packed.shape[0] // groups
    model_width = merge.shape[2]
    has_prev, has_next = group > 0, group < groups - 1

    barrier = pltpu.get_barrier_semaphore()
    pl.semaphore_signal(barrier, inc=1, device_id=(group, beside), device_id_type=MESH)
    for step in range(1, groups):
        partner = lax.rem(group + step, groups)
        pl.semaphore_signal(barrier, inc=1, device_id=(partner, core), device_id_type=MESH)
    loads = [pltpu.make_async_copy(qkv_hbm.at[i], qkv.at[i], load_sems.at[i]) for i in range(3)]
    loads[1].start()
    loads[0].start()
    loads[2].start()
    fetches = [
        pltpu.make_async_copy(merge_hbm.at[j], merge.at[j], merge_sems.at[j]) for j in range(WIN)
    ]
    fetches.append(pltpu.make_async_copy(next_hbm, next_weight, next_sem))
    for fetch in fetches:
        fetch.start()

    def along(kind, side, source, target):
        partner = lax.rem(group + groups - 1, groups) if side == 0 else lax.rem(group + 1, groups)
        return pltpu.make_async_remote_copy(
            src_ref=source,
            dst_ref=target.at[1 - side],
            send_sem=next_send.at[kind, side],
            recv_sem=next_recv.at[kind, 1 - side],
            device_id=(partner, core),
            device_id_type=MESH,
        )

    def across(kind, source, target):
        return pltpu.make_async_remote_copy(
            src_ref=source,
            dst_ref=target,
            send_sem=swap_send.at[kind],
            recv_sem=swap_recv.at[kind],
            device_id=(group, beside),
            device_id_type=MESH,
        )

    query_moves = [
        along(0, side, qkv_hbm.at[0, :, pl.ds(side * (row_len - sent), sent)], query_in)
        for side in range(2)
    ]
    stats_moves = [along(1, side, stats_out.at[side], stats_in) for side in range(2)]
    back_moves = [along(2, side, back_out.at[side], back_in) for side in range(2)]
    part_moves = [along(3, side, part_out.at[side], part_in) for side in range(2)]
    exists = [has_prev, has_next]

    def begin(moves, side):
        pl.when(exists[side])(lambda: moves[side].start())

    def landed(moves, slot):
        pl.when(exists[slot])(lambda: moves[1 - slot].wait_recv())

    def left(moves, side):
        pl.when(exists[side])(lambda: moves[side].wait_send())

    for slot in range(2):
        @pl.when(jnp.logical_not(exists[slot]))
        def _():
            query_in[slot] = jnp.zeros(query_in.shape[1:], query_in.dtype)
            stats_in[slot] = jnp.full(stats_in.shape[1:], -NEG, jnp.float32)
            back_in[slot] = jnp.full(back_in.shape[1:], NEG, jnp.float32)
            part_in[slot] = jnp.zeros(part_in.shape[1:], part_in.dtype)

    gain, bias = small_ref[:, :model_width], small_ref[:, model_width : 2 * model_width]
    ids_at = 2 * model_width
    seg = small_ref[:, ids_at : ids_at + row_len].astype(jnp.int32)
    owners_at = ids_at + row_len
    owner_row = small_ref[:, owners_at : owners_at + groups].astype(jnp.int32)
    link = small_ref[:, owners_at + groups : owners_at + groups + 1]
    bit = jnp.left_shift(1, lax.broadcasted_iota(jnp.int32, (PACK, 1), 0))
    real = lax.broadcasted_iota(jnp.int32, (PACK, 1), 0) < 8

    def code_of(ids, size):
        sign = jnp.where(jnp.bitwise_and(ids, bit) != 0, size, -size)
        return jnp.where(real, sign, 0.0).astype(jnp.bfloat16)

    pl.semaphore_wait(barrier, groups)
    begin(query_moves, 0)
    begin(query_moves, 1)

    key_code = code_of(seg, 1.0)
    key_fill = jnp.zeros((TILE - SPAN - PACK, row_len), jnp.bfloat16)
    loads[1].wait()
    for head in range(heads):
        start = head * DH // PACK * PACK
        block = jnp.concatenate([qkv[1, start : start + SPAN, :], key_code, key_fill], axis=0).T
        spread_keys[head, :, :TILE] = block
        spread_keys[head, :, TILE:] = block
    loads[2].wait()
    span_row = lax.broadcasted_iota(jnp.int32, (SPAN, 1), 0)
    for head in range(heads):
        start = head * DH // PACK * PACK
        spare = span_row < SPAN - DH if head % 2 == 1 else span_row >= DH
        value = qkv[2, start : start + SPAN, :].astype(jnp.float32)
        spread_values[head] = jnp.where(spare, 1.0, value).astype(jnp.bfloat16)
    loads[0].wait()

    @pl.loop(0, parts)
    def _(part):
        at = pl.multiple_of(part * sent, sent)
        mixed, stats = soft_heads(
            heads,
            lambda a, b: qkv[0, a:b, pl.ds(at, sent)],
            code_of(
                small_ref[:, pl.ds(pl.multiple_of(ids_at + at, TILE), sent)].astype(jnp.int32), CODE
            ),
            lambda head: spread_keys[head],
            lambda head: spread_values[head],
        )
        local_mixed[part] = mixed
        local_stats[part] = stats

    first_id, last_id = seg[:, :1], seg[:, row_len - 1 :]
    link_open = jnp.logical_and(link > 0, has_next)
    in_first = seg[:, :sent] == first_id
    in_last = jnp.logical_and(seg[:, row_len - sent :] == last_id, link_open)
    inside = [in_first, in_last]
    stats_out[0] = jnp.where(in_first, local_stats[0], -NEG)
    stats_out[1] = jnp.where(in_last, local_stats[parts - 1], -NEG)
    begin(stats_moves, 0)
    begin(stats_moves, 1)

    ordered = lax.broadcasted_iota(jnp.int32, (sent, sent), 0)
    ordered = (ordered % tokens) * WIN + ordered // tokens
    order = (ordered == lax.broadcasted_iota(jnp.int32, (sent, sent), 1)).astype(jnp.float32)
    order = order.astype(jnp.bfloat16)

    def turn(mixed, target, at):
        turned = lax.dot_general(
            order,
            mixed.astype(jnp.bfloat16),
            (((1,), (1,)), ((), ())),
            preferred_element_type=jnp.float32,
        ).astype(jnp.bfloat16)
        for j in range(WIN):
            target[j, at : at + tokens, :] = turned[j * tokens : (j + 1) * tokens]

    def merge_rows(attended):
        merged = jnp.dot(attended[0], merge[0], preferred_element_type=jnp.float32)
        for j in range(1, WIN):
            merged += jnp.dot(attended[j], merge[j], preferred_element_type=jnp.float32)
        return merged

    def scaled_heads(mixed, scale):
        return jnp.concatenate(
            [mixed[h * DH : (h + 1) * DH] * scale[h : h + 1] for h in range(heads)], axis=0
        )

    for part in range(1, parts - 1):
        turn(local_mixed[part], attended_mid, (part - 1) * tokens)
    for fetch in fetches[:WIN]:
        fetch.wait()
    mid_part[...] = merge_rows(attended_mid)
    mid_move = across(0, mid_part, mid_swap)
    mid_move.start()
    for side in range(2):
        keys_at = side * (row_len - sent)
        code = code_of(first_id if side == 0 else last_id, CODE)
        landed(query_moves, side)
        mixed, stats = soft_heads(
            heads,
            lambda a, b: query_in[side, a:b, :],
            jnp.broadcast_to(code.astype(jnp.float32), (PACK, sent)).astype(jnp.bfloat16),
            lambda head: spread_keys[head, keys_at : keys_at + sent, :],
            lambda head: spread_values[head, :, keys_at : keys_at + sent],
        )
        if side == 1:
            stats = jnp.where(link_open, stats, NEG)
        far_mixed[side] = mixed
        far_stats[side] = stats
        back_out[side] = stats
        begin(back_moves, side)
    for side in range(2):
        landed(stats_moves, side)
        share = 1.0 / (1.0 + jnp.exp2(stats_in[side] - far_stats[side]))
        turn(scaled_heads(far_mixed[side], share), attended_far, side * tokens)
    far_merged = merge_rows(attended_far)
    half = tokens // 2
    for side in range(2):
        for part in range(2):
            piece = far_merged[side * tokens + part * half : side * tokens + (part + 1) * half]
            far_part[part, side] = piece
            far_low[part, side] = piece.astype(jnp.bfloat16)
    far_move = across(1, far_low.at[beside], far_swap)
    far_move.start()
    far_move.wait_recv()
    for side in range(2):
        part_out[side] = (far_part[core, side] + far_swap[side].astype(jnp.float32)).astype(jnp.bfloat16)
        begin(part_moves, side)

    for side in range(2):
        landed(back_moves, side)
        back = jnp.where(inside[side], back_in[side], NEG)
        place_at = side * (parts - 1)
        share = 1.0 / (1.0 + jnp.exp2(back - local_stats[place_at]))
        turn(scaled_heads(local_mixed[place_at], share), attended_edge, side * tokens)
    edge_merged = merge_rows(attended_edge)
    for side in range(2):
        for part in range(2):
            at = side * tokens + part * half
            edge_part[part, side] = edge_merged[at : at + half]

    edge_move = across(2, edge_part, edge_swap)
    edge_move.start()

    def norm(merged):
        mean = jnp.sum(merged, axis=1, keepdims=True) / model_width
        variance = jnp.sum(merged * merged, axis=1, keepdims=True) / model_width - mean * mean
        value = (merged - mean) * lax.rsqrt(variance + EPS) * gain + bias
        return value.astype(jnp.bfloat16)

    mid_move.wait_recv()
    normed[tokens : (parts - 1) * tokens, :] = norm(mid_part[...] + mid_swap[...])

    blocks, merged_rows = groups, packed.shape[0]
    same = lax.broadcasted_iota(jnp.int32, (blocks, blocks), 0)
    same = same == lax.broadcasted_iota(jnp.int32, (blocks, blocks), 1)
    owner_col = jnp.sum(jnp.where(same, owner_row, 0), axis=1, keepdims=True)
    block_row = lax.broadcasted_iota(jnp.int32, (blocks, merged_rows), 0)
    block_of = lax.broadcasted_iota(jnp.int32, (blocks, merged_rows), 1) // rows
    owner_of = jnp.sum(jnp.where(block_row == block_of, owner_col, 0), axis=0, keepdims=True)
    earlier = jnp.logical_and(owner_col == owner_of, block_row < block_of)
    rank = jnp.sum(jnp.where(earlier, 1, 0), axis=0, keepdims=True)
    token = lax.broadcasted_iota(jnp.int32, (1, merged_rows), 1)
    target = jnp.where(rank == core, owner_of * rows + token % rows, -1)
    place = lax.broadcasted_iota(jnp.int32, (merged_rows, merged_rows), 0)
    place = jnp.where(place == target, 1.0, 0.0).astype(jnp.bfloat16)

    edge_move.wait_recv()
    share_moves = [across(3 + side, part_in.at[side], part_far.at[side]) for side in range(2)]
    for side in range(2):
        landed(part_moves, side)
        share_moves[side].start()
        at = pl.multiple_of(side * (parts - 1) * tokens + core * half, half)
        value = edge_part[core, side] + edge_swap[core, side] + part_in[side].astype(jnp.float32)
        normed[pl.ds(at, half), :] = norm(value)
    for side in range(2):
        share_moves[side].wait_recv()
        at = pl.multiple_of(side * (parts - 1) * tokens + beside * half, half)
        value = edge_part[beside, side] + edge_swap[beside, side] + part_far[side].astype(jnp.float32)
        normed[pl.ds(at, half), :] = norm(value)
    packed[...] = jnp.dot(place, normed[...], preferred_element_type=jnp.float32).astype(jnp.bfloat16)

    def outgoing(partner):
        return pltpu.make_async_remote_copy(
            src_ref=packed.at[pl.ds(pl.multiple_of(partner * rows, rows), rows), :],
            dst_ref=routed_ref.at[group, core],
            send_sem=send_sems.at[partner],
            recv_sem=recv_sems.at[group],
            device_id=(partner, core),
            device_id_type=MESH,
        )

    def incoming(source):
        return pltpu.make_async_remote_copy(
            src_ref=packed.at[pl.ds(0, rows), :],
            dst_ref=routed_ref.at[source, core],
            send_sem=send_sems.at[source],
            recv_sem=recv_sems.at[source],
            device_id=(source, core),
            device_id_type=MESH,
        )

    def handed(source, whose):
        return pltpu.make_async_remote_copy(
            src_ref=routed_ref.at[source, whose],
            dst_ref=routed_ref.at[source, whose],
            send_sem=over_sems.at[source],
            recv_sem=back_sems.at[source],
            device_id=(group, beside),
            device_id_type=MESH,
        )

    bulk = groups // 2
    mine = group // bulk
    for step in range(bulk):
        outgoing((1 - mine) * bulk + lax.rem(group + step, bulk)).start()
    for step in range(1, bulk):
        outgoing(mine * bulk + lax.rem(group + step, bulk)).start()
    own = pl.multiple_of(group * rows, rows)
    routed_ref[group, core] = packed[pl.ds(own, rows), :]
    handed(group, core).start()
    fetches[WIN].wait()
    span = bulk * CAP * rows

    @pl.loop(0, 2)
    def _(phase):
        half_at = lax.rem(mine + phase, 2)
        for step in range(bulk):
            source = half_at * bulk + lax.rem(group + bulk - step, bulk)

            @pl.when(source != group)
            def _():
                incoming(source).wait_recv()
                handed(source, core).start()

        for step in range(bulk):
            handed(half_at * bulk + step, beside).wait_recv()
        arrived = routed_ref[pl.ds(half_at * bulk, bulk)]
        routed_turned[...] = arrived.reshape(span, model_width).T
        projected = jnp.dot(next_weight[...], routed_turned[...], preferred_element_type=jnp.float32)
        out_ref[:, pl.ds(pl.multiple_of(half_at * span, span), span)] = projected.astype(jnp.bfloat16)

    for side in range(2):
        for moves in (query_moves, stats_moves, back_moves, part_moves):
            left(moves, side)
    for move in (mid_move, far_move, edge_move, *share_moves):
        move.wait_send()
    for step in range(groups):
        handed(step, core).wait_send()
    for step in range(1, groups):
        outgoing(lax.rem(group + step, groups)).wait_send()


def encode(qkv, merge_weight, small, next_weight, groups):
    width, row_len = qkv.shape[1:]
    model_width = merge_weight.shape[2]
    heads = width // DH
    parts = 4
    sent = row_len // parts
    tokens = sent // WIN
    merged_rows = row_len // WIN
    rows = merged_rows // groups
    slots = groups * CAP * rows
    vmem = pl.BlockSpec(memory_space=pltpu.VMEM)
    hbm = pl.BlockSpec(memory_space=pltpu.HBM)
    low, full = jnp.bfloat16, jnp.float32
    return pl.pallas_call(
        encoder_kernel,
        out_shape=jax.ShapeDtypeStruct((next_weight.shape[0], slots), low),
        in_specs=[hbm, hbm, vmem, hbm],
        out_specs=vmem,
        scratch_shapes=[
            pltpu.VMEM((groups, CAP, rows, model_width), low),
            pltpu.VMEM(next_weight.shape, low),
            pltpu.VMEM((model_width, slots // 2), low),
            pltpu.VMEM(qkv.shape, low),
            pltpu.VMEM(merge_weight.shape, low),
            pltpu.VMEM((heads, row_len, 2 * TILE), low),
            pltpu.VMEM((heads, SPAN, row_len), low),
            pltpu.VMEM((parts, width, sent), full),
            pltpu.VMEM((parts, heads, sent), full),
            pltpu.VMEM((2, width, sent), full),
            pltpu.VMEM((2, heads, sent), full),
            pltpu.VMEM((2, width, sent), low),
            pltpu.VMEM((2, heads, sent), full),
            pltpu.VMEM((2, heads, sent), full),
            pltpu.VMEM((2, heads, sent), full),
            pltpu.VMEM((2, heads, sent), full),
            pltpu.VMEM((WIN, 2 * tokens, width), low),
            pltpu.VMEM((WIN, 2 * tokens, width), low),
            pltpu.VMEM((WIN, 2 * tokens, width), low),
            pltpu.VMEM((2, 2, tokens // 2, model_width), full),
            pltpu.VMEM((2, 2, tokens // 2, model_width), low),
            pltpu.VMEM((2, tokens // 2, model_width), low),
            pltpu.VMEM((2, tokens // 2, model_width), low),
            pltpu.VMEM((2, tokens // 2, model_width), low),
            pltpu.VMEM((2 * tokens, model_width), full),
            pltpu.VMEM((2 * tokens, model_width), full),
            pltpu.VMEM((2, tokens // 2, model_width), low),
            pltpu.VMEM((2, 2, tokens // 2, model_width), full),
            pltpu.VMEM((2, 2, tokens // 2, model_width), full),
            pltpu.VMEM((merged_rows, model_width), low),
            pltpu.VMEM((merged_rows, model_width), low),
            pltpu.SemaphoreType.DMA((3,)),
            pltpu.SemaphoreType.DMA((WIN,)),
            pltpu.SemaphoreType.DMA,
            pltpu.SemaphoreType.DMA((4, 2)),
            pltpu.SemaphoreType.DMA((4, 2)),
            pltpu.SemaphoreType.DMA((5,)),
            pltpu.SemaphoreType.DMA((5,)),
            pltpu.SemaphoreType.DMA((groups,)),
            pltpu.SemaphoreType.DMA((groups,)),
            pltpu.SemaphoreType.DMA((groups,)),
            pltpu.SemaphoreType.DMA((groups,)),
        ],
        compiler_params=pltpu.CompilerParams(
            vmem_limit_bytes=51 << 20, collective_id=0, has_side_effects=True
        ),
        name="encode",
    )(qkv, merge_weight, small, next_weight)


def body(qkv, segments, links, owners, merge_weight, norm_gain, norm_bias, next_weight):
    row_len = qkv.shape[1]
    model_width = norm_gain.shape[0]
    tp_size = lax.axis_size("tp")
    turned = jnp.swapaxes(qkv, 1, 2)
    group_count = lax.axis_size("grp")
    owner_ids = owners[0, :, 0]
    block_count = owner_ids.shape[0]
    if tp_size == 2 and block_count == group_count:
        small = [norm_gain, norm_bias, segments[0], owner_ids, links]
        small = jnp.concatenate([part.astype(jnp.float32) for part in small])
        small = jnp.pad(small, (0, -small.shape[0] % TILE))[None]
        projected = encode(turned, merge_weight, small, next_weight.T, group_count)
        return projected.T[None]
    seg_ids = segments[0]
    linked = links[0] > 0
    sent = row_len // 4
    last_flag = jnp.logical_and(seg_ids == seg_ids[row_len - 1], linked)[row_len - sent :]
    first_flag = (seg_ids == seg_ids[0])[:sent]

    def payload(pairs, flag):
        mark = jnp.broadcast_to(flag.astype(jnp.bfloat16)[None, None, :], (2, PACK, sent))
        return jnp.concatenate([pairs, mark], axis=1)

    prev = shifted(payload(turned[1:3, :, row_len - sent :], last_flag), "grp", 1)
    following = shifted(payload(turned[1:3, :, :sent], first_flag), "grp", -1)
    middle = run_attention(False, turned, segments, merge_weight, sent, None)
    partial_sum = run_attention(
        True, turned, segments, merge_weight, sent, (links, prev, following, middle)
    )
    merged_rows = row_len // WIN

    block_rows = merged_rows // block_count
    block_index = jnp.arange(block_count)
    earlier = block_index[:, None] > block_index[None, :]
    slot_rank = jnp.sum(
        jnp.logical_and(owner_ids[:, None] == owner_ids[None, :], earlier).astype(jnp.int32), axis=1
    )
    slots = group_count * CAP * block_rows

    target = (owner_ids * CAP + slot_rank)[:, None] * block_rows
    target = (target + jnp.arange(block_rows)[None, :]).reshape(merged_rows)
    merged = lax.psum(partial_sum, "tp")
    mean = jnp.mean(merged, axis=1, keepdims=True)
    variance = jnp.mean(merged * merged, axis=1, keepdims=True) - mean * mean
    normed = (merged - mean) * lax.rsqrt(variance + EPS) * norm_gain + norm_bias
    normed = normed.astype(jnp.bfloat16)
    placing = (jnp.arange(slots)[:, None] == target[None, :]).astype(jnp.bfloat16)
    packed = jnp.dot(placing, normed, preferred_element_type=jnp.float32).astype(jnp.bfloat16)
    packed = packed.reshape(group_count, CAP * block_rows, model_width)
    routed = lax.all_to_all(packed, "grp", split_axis=0, concat_axis=0, tiled=True)
    routed = routed.reshape(slots, model_width)
    projected = jnp.dot(routed, next_weight, preferred_element_type=jnp.float32)
    return projected.astype(jnp.bfloat16)[None]


def solution(mesh):
    placed = (
        P(None, "grp", "tp"),
        P("grp", None),
        P("grp"),
        P("grp", None, None),
        P(None, "tp", None),
        P(),
        P(),
        P(None, "tp"),
    )
    return jax.shard_map(
        body, mesh=mesh, in_specs=placed, out_specs=P("grp", None, "tp"), check_vma=False
    )
```

```python
import functools
import math

import jax
import jax.numpy as jnp
from jax import lax
from jax.experimental import pallas as pl
from jax.experimental.pallas import tpu as pltpu
from jax.sharding import PartitionSpec as P

DH = 88
WIN = 4
CAP = 2
TILE = 128
PACK = 16
EPS = 1e-05
NEG = -1e30
MESH = pl.DeviceIdType.MESH
SPAN = 96
CODE = 640.0
SCALE2 = math.log2(math.e) / math.sqrt(DH)


def shifted(block, axis, distance):
    devices = range(lax.axis_size(axis))
    route = [(i - distance, i) for i in devices if i - distance in devices]
    return lax.ppermute(block, axis, route)


def attend_heads(width, read_query, key_parts, bias_parts, value_parts, together=4):
    pieces = []
    for base in range(0, width // DH, together):
        lows = [head * DH for head in range(base, min(base + together, width // DH))]
        scores = []
        for low in lows:
            start, stop = low // TILE * TILE, min(width, -(-(low + DH) // TILE) * TILE)
            row = start + lax.broadcasted_iota(jnp.int32, (stop - start, 1), 0)
            inside = jnp.logical_and(row >= low, row < low + DH)
            query = read_query(start, stop)
            query = jnp.where(inside, query.astype(jnp.float32), 0.0).astype(jnp.bfloat16)
            scores.append(
                [jnp.dot(keys(start, stop), query, preferred_element_type=jnp.float32) for keys in key_parts]
            )
        scores = [[part * SCALE2 + bias for part, bias in zip(parts, bias_parts)] for parts in scores]
        tops = [
            functools.reduce(jnp.maximum, [jnp.max(part, axis=0, keepdims=True) for part in parts])
            for parts in scores
        ]
        weights = [[jnp.exp2(part - top) for part in parts] for parts, top in zip(scores, tops)]
        scales = [
            1.0 / functools.reduce(jnp.add, [jnp.sum(part, axis=0, keepdims=True) for part in parts])
            for parts in weights
        ]
        weights = [
            [(part * scale).astype(jnp.bfloat16) for part in parts] for parts, scale in zip(weights, scales)
        ]
        for low, parts in zip(lows, weights):
            start, stop = low // PACK * PACK, -(-(low + DH) // PACK) * PACK
            terms = [
                jnp.dot(values(start, stop), part, preferred_element_type=jnp.float32)
                for part, values in zip(parts, value_parts)
            ]
            pieces.append(functools.reduce(jnp.add, terms)[low - start : low - start + DH])
    return jnp.concatenate(pieces, axis=0)


def attention_kernel(edge, row_len, width, sent, *refs):
    if edge:
        seg_smem, qkv_hbm, seg_row, seg_col, merge_hbm, links, prev, following, middle, out = refs[:10]
    else:
        seg_smem, qkv_hbm, seg_row, seg_col, merge_hbm, out = refs[:6]
    attended, merge_vmem, merge_sem, qkv, qkv_sem, turned_keys, turned_sides = refs[-7:]
    tiles = row_len // TILE
    edge_tiles = sent // TILE
    tokens = TILE // WIN
    fetch = pltpu.make_async_copy(merge_hbm, merge_vmem, merge_sem)
    load = pltpu.make_async_copy(qkv_hbm, qkv, qkv_sem)
    load.start()
    fetch.start()
    if edge:
        for side, source in enumerate((prev, following)):
            for at in range(0, sent, TILE):
                turned_sides[side, at : at + TILE, :] = source[0, :width, at : at + TILE].T
    load.wait()

    @pl.loop(0, tiles)
    def _(tile):
        at = pl.multiple_of(tile * TILE, TILE)
        turned_keys[pl.ds(at, TILE), :] = qkv[1, :, pl.ds(at, TILE)].T

    ordered = lax.broadcasted_iota(jnp.int32, (TILE, TILE), 0)
    ordered = (ordered % tokens) * WIN + ordered // tokens
    order = (ordered == lax.broadcasted_iota(jnp.int32, (TILE, TILE), 1)).astype(jnp.float32)
    order = order.astype(jnp.bfloat16)

    def one(tile, out_row, neighbour):
        first = seg_smem[0, tile * TILE]
        last = seg_smem[0, tile * TILE + TILE - 1]
        begin, stop = jnp.int32(0), jnp.int32(0)
        for other in range(tiles):
            begin += (seg_smem[0, other * TILE + TILE - 1] < first).astype(jnp.int32)
            stop += (seg_smem[0, other * TILE] <= last).astype(jnp.int32)
        needed = stop - begin
        query_at = pl.multiple_of(tile * TILE, TILE)
        query_ids = seg_row[pl.ds(tile, 1), :]

        def run(count):
            key_at = pl.multiple_of(jnp.minimum(begin, tiles - count) * TILE, TILE)
            key_ids = seg_col[pl.ds(key_at, count * TILE), :]
            bias_parts = [jnp.where(key_ids == query_ids, 0.0, NEG)]
            key_parts = [lambda a, b: turned_keys[pl.ds(key_at, count * TILE), a:b]]
            value_parts = [lambda a, b: qkv[2, a:b, pl.ds(key_at, count * TILE)]]
            if neighbour is not None:
                side, source, segment, open_link = neighbour
                marks = jnp.transpose(source[0, width : width + PACK, :].astype(jnp.float32))[:, :1]
                wanted = jnp.logical_and(query_ids == segment, open_link).astype(jnp.float32)
                bias_parts.append(jnp.where(marks * wanted > 0.5, 0.0, NEG))
                key_parts.append(lambda a, b: turned_sides[side, :, a:b])
                value_parts.append(lambda a, b: source[1, a:b, :])
            mixed = attend_heads(
                width,
                lambda a, b: qkv[0, a:b, pl.ds(query_at, TILE)],
                key_parts,
                bias_parts,
                value_parts,
            )
            turned = lax.dot_general(
                order,
                mixed.astype(jnp.bfloat16),
                (((1,), (1,)), ((), ())),
                preferred_element_type=jnp.float32,
            ).astype(jnp.bfloat16)
            for j in range(WIN):
                attended[j, pl.ds(out_row, tokens), :] = turned[j * tokens : (j + 1) * tokens]

        sizes = [size for size in (2, 3, 4) if size < tiles] + [tiles]
        floor = 0
        for size in sizes:
            pl.when(jnp.logical_and(needed > floor, needed <= size))(functools.partial(run, size))
            floor = size

    if edge:
        @pl.loop(0, edge_tiles)
        def _(tile):
            one(tile, pl.multiple_of(tile * tokens, tokens), (0, prev, seg_smem[0, 0], True))

        @pl.loop(0, edge_tiles)
        def _(step):
            one(
                tiles - edge_tiles + step,
                pl.multiple_of((edge_tiles + step) * tokens, tokens),
                (1, following, seg_smem[0, row_len - 1], links[0] > 0),
            )
    else:
        @pl.loop(edge_tiles, tiles - edge_tiles)
        def _(tile):
            one(tile, pl.multiple_of((tile - edge_tiles) * tokens, tokens), None)

    fetch.wait()
    merged = jnp.dot(attended[0], merge_vmem[0], preferred_element_type=jnp.float32)
    for j in range(1, WIN):
        merged += jnp.dot(attended[j], merge_vmem[j], preferred_element_type=jnp.float32)
    if edge:
        half = merged.shape[0] // 2
        out[:half, :] = merged[:half]
        out[half : half + middle.shape[0], :] = middle[...]
        out[half + middle.shape[0] :, :] = merged[half:]
    else:
        out[...] = merged


def run_attention(edge, qkv, segments, merge_weight, sent, extra):
    width, row_len = qkv.shape[1:]
    model_width = merge_weight.shape[2]
    rows = 2 * sent if edge else row_len - 2 * sent
    smem = pl.BlockSpec(memory_space=pltpu.SMEM)
    vmem = pl.BlockSpec(memory_space=pltpu.VMEM)
    operands = [
        segments,
        qkv,
        segments.reshape(row_len // TILE, TILE),
        segments.reshape(row_len, 1),
        merge_weight,
    ]
    hbm = pl.BlockSpec(memory_space=pltpu.HBM)
    specs = [smem, hbm, vmem, vmem, hbm]
    if edge:
        operands += list(extra)
        specs += [smem, vmem, vmem, vmem]
    out_rows = row_len // WIN if edge else rows // WIN
    return pl.pallas_call(
        functools.partial(attention_kernel, edge, row_len, width, sent),
        out_shape=jax.ShapeDtypeStruct((out_rows, model_width), jnp.float32),
        in_specs=specs,
        out_specs=vmem,
        scratch_shapes=[
            pltpu.VMEM((WIN, rows // WIN, width), jnp.bfloat16),
            pltpu.VMEM(merge_weight.shape, jnp.bfloat16),
            pltpu.SemaphoreType.DMA,
            pltpu.VMEM(qkv.shape, jnp.bfloat16),
            pltpu.SemaphoreType.DMA,
            pltpu.VMEM((row_len, width), jnp.bfloat16),
            pltpu.VMEM((2, sent, width), jnp.bfloat16),
        ],
        compiler_params=pltpu.CompilerParams(vmem_limit_bytes=40 << 20),
        cost_estimate=pl.CostEstimate(
            flops=rows * 512 * width * 6, bytes_accessed=qkv.size * 2, transcendentals=rows * 512 * 8
        ),
        name="edge_attention" if edge else "middle_attention",
    )(*operands)


def spread_query(query, odd, code):
    row = lax.broadcasted_iota(jnp.int32, query.shape, 0)
    inside = row >= SPAN - DH if odd else row < DH
    scaled = jnp.where(inside, query.astype(jnp.float32) * SCALE2, 0.0)
    high = scaled.astype(jnp.bfloat16)
    low = (scaled - high.astype(jnp.float32)).astype(jnp.bfloat16)
    columns = query.shape[1]
    return jnp.concatenate(
        [high, code, jnp.zeros((TILE - SPAN - PACK, columns), jnp.bfloat16)]
        + [low, jnp.zeros((TILE - SPAN, columns), jnp.bfloat16)],
        axis=0,
    )


def soft_heads(units, together):
    pieces, tops = [], []
    for base in range(0, len(units), together):
        group = units[base : base + together]
        scores = []
        for head, read_query, code, read_keys, _ in group:
            start = head * DH // PACK * PACK
            spread = spread_query(read_query(start, start + SPAN), head % 2 == 1, code)
            scores.append(jnp.dot(read_keys(head), spread, preferred_element_type=jnp.float32))
        maxima = [jnp.max(score, axis=0, keepdims=True) for score in scores]
        weights = [jnp.exp2(score - top).astype(jnp.bfloat16) for score, top in zip(scores, maxima)]
        for (head, _, _, _, read_values), top, weight in zip(group, maxima, weights):
            mixed = jnp.dot(read_values(head), weight, preferred_element_type=jnp.float32)
            if head % 2 == 1:
                total, mixed = mixed[:1], mixed[SPAN - DH :]
            else:
                total, mixed = mixed[DH : DH + 1], mixed[:DH]
            pieces.append(mixed * (1.0 / total))
            tops.append(top + jnp.log2(total))
    return pieces, tops


def encoder_kernel(
    qkv_hbm,
    merge_hbm,
    gain_ref,
    ids_ref,
    next_hbm,
    out_ref,
    routed_ref,
    next_weight,
    routed_turned,
    qkv,
    merge,
    spread_keys,
    spread_values,
    local_mixed,
    local_stats,
    far_mixed,
    far_stats,
    query_in,
    stats_out,
    stats_in,
    back_out,
    back_in,
    attended_mid,
    attended_far,
    attended_edge,
    far_part,
    far_low,
    far_swap,
    part_out,
    part_in,
    mid_part,
    mid_swap,
    part_far,
    edge_part,
    edge_swap,
    normed,
    packed,
    load_sems,
    merge_sems,
    next_sem,
    next_send,
    next_recv,
    swap_send,
    swap_recv,
    send_sems,
    recv_sems,
    over_sems,
    back_sems,
):
    group, core = lax.axis_index("grp"), lax.axis_index("tp")
    groups = lax.axis_size("grp")
    beside = 1 - core
    width, row_len = qkv.shape[1:]
    heads = width // DH
    sent = query_in.shape[2]
    parts = row_len // sent
    tokens = sent // WIN
    rows = packed.shape[0] // groups
    model_width = merge.shape[2]
    has_prev, has_next = group > 0, group < groups - 1

    barrier = pltpu.get_barrier_semaphore()
    pl.semaphore_signal(barrier, inc=1, device_id=(group, beside), device_id_type=MESH)
    for step in range(1, groups):
        partner = lax.rem(group + step, groups)
        pl.semaphore_signal(barrier, inc=1, device_id=(partner, core), device_id_type=MESH)
    loads = [pltpu.make_async_copy(qkv_hbm.at[i], qkv.at[i], load_sems.at[i]) for i in range(3)]
    loads[1].start()
    loads[0].start()
    loads[2].start()
    fetches = [
        pltpu.make_async_copy(merge_hbm.at[j], merge.at[j], merge_sems.at[j]) for j in range(WIN)
    ]
    fetches.append(pltpu.make_async_copy(next_hbm, next_weight, next_sem))

    def along(kind, side, source, target):
        partner = lax.rem(group + groups - 1, groups) if side == 0 else lax.rem(group + 1, groups)
        return pltpu.make_async_remote_copy(
            src_ref=source,
            dst_ref=target.at[1 - side],
            send_sem=next_send.at[kind, side],
            recv_sem=next_recv.at[kind, 1 - side],
            device_id=(partner, core),
            device_id_type=MESH,
        )

    def across(kind, source, target):
        return pltpu.make_async_remote_copy(
            src_ref=source,
            dst_ref=target,
            send_sem=swap_send.at[kind],
            recv_sem=swap_recv.at[kind],
            device_id=(group, beside),
            device_id_type=MESH,
        )

    query_moves = [
        along(0, side, qkv_hbm.at[0, :, pl.ds(side * (row_len - sent), sent)], query_in)
        for side in range(2)
    ]
    stats_moves = [along(1, side, stats_out.at[side], stats_in) for side in range(2)]
    back_moves = [along(2, side, back_out.at[side], back_in) for side in range(2)]
    part_moves = [along(3, side, part_out.at[side], part_in) for side in range(2)]
    exists = [has_prev, has_next]

    def begin(moves, side):
        pl.when(exists[side])(lambda: moves[side].start())

    def landed(moves, slot):
        pl.when(exists[slot])(lambda: moves[1 - slot].wait_recv())

    def left(moves, side):
        pl.when(exists[side])(lambda: moves[side].wait_send())

    for slot in range(2):
        @pl.when(jnp.logical_not(exists[slot]))
        def _():
            query_in[slot] = jnp.zeros(query_in.shape[1:], query_in.dtype)
            stats_in[slot] = jnp.full(stats_in.shape[1:], -NEG, jnp.float32)
            back_in[slot] = jnp.full(back_in.shape[1:], NEG, jnp.float32)
            part_in[slot] = jnp.zeros(part_in.shape[1:], part_in.dtype)

    gain, bias = gain_ref[:, :model_width], gain_ref[:, model_width:]
    ids_at = 0

    def small_ids(where):
        return ids_ref[:, where]

    seg = small_ids(slice(ids_at, ids_at + row_len))
    owners_at = ids_at + row_len
    owner_row = small_ids(slice(owners_at, owners_at + groups))
    link = ids_ref[:, owners_at + groups : owners_at + groups + 1]
    bit = jnp.left_shift(1, lax.broadcasted_iota(jnp.int32, (PACK, 1), 0))
    real = lax.broadcasted_iota(jnp.int32, (PACK, 1), 0) < 8

    def code_of(ids, size):
        sign = jnp.where(jnp.bitwise_and(ids, bit) != 0, size, -size)
        return jnp.where(real, sign, 0.0).astype(jnp.bfloat16)

    pl.semaphore_wait(barrier, groups)
    begin(query_moves, 0)
    begin(query_moves, 1)
    for fetch in fetches:
        fetch.start()

    key_code = code_of(seg, 1.0)
    key_fill = jnp.zeros((TILE - SPAN - PACK, row_len), jnp.bfloat16)
    loads[1].wait()
    for head in range(heads):
        start = head * DH // PACK * PACK
        block = jnp.concatenate([qkv[1, start : start + SPAN, :], key_code, key_fill], axis=0).T
        spread_keys[head, :, :TILE] = block
        spread_keys[head, :, TILE:] = block
    loads[2].wait()
    span_row = lax.broadcasted_iota(jnp.int32, (SPAN, 1), 0)
    for head in range(heads):
        start = head * DH // PACK * PACK
        spare = span_row < SPAN - DH if head % 2 == 1 else span_row >= DH
        value = qkv[2, start : start + SPAN, :].astype(jnp.float32)
        spread_values[head] = jnp.where(spare, 1.0, value).astype(jnp.bfloat16)
    loads[0].wait()

    @pl.loop(0, parts)
    def _(part):
        at = pl.multiple_of(part * sent, sent)
        code = code_of(small_ids(pl.ds(pl.multiple_of(ids_at + at, TILE), sent)), CODE)
        units = [
            (
                head,
                lambda a, b: qkv[0, a:b, pl.ds(at, sent)],
                code,
                lambda head: spread_keys[head],
                lambda head: spread_values[head],
            )
            for head in range(heads)
        ]
        pieces, tops = soft_heads(units, 8)
        local_mixed[part] = jnp.concatenate(pieces, axis=0)
        local_stats[part] = jnp.concatenate(tops, axis=0)

    first_id, last_id = seg[:, :1], seg[:, row_len - 1 :]
    link_open = jnp.logical_and(link > 0, has_next)
    in_first = seg[:, :sent] == first_id
    in_last = jnp.logical_and(seg[:, row_len - sent :] == last_id, link_open)
    inside = [in_first, in_last]
    stats_out[0] = jnp.where(in_first, local_stats[0], -NEG)
    stats_out[1] = jnp.where(in_last, local_stats[parts - 1], -NEG)
    begin(stats_moves, 0)
    begin(stats_moves, 1)

    ordered = lax.broadcasted_iota(jnp.int32, (sent, sent), 0)
    ordered = (ordered % tokens) * WIN + ordered // tokens
    order = (ordered == lax.broadcasted_iota(jnp.int32, (sent, sent), 1)).astype(jnp.float32)
    order = order.astype(jnp.bfloat16)

    def turn(mixed, target, at):
        turned = lax.dot_general(
            order,
            mixed.astype(jnp.bfloat16),
            (((1,), (1,)), ((), ())),
            preferred_element_type=jnp.float32,
        ).astype(jnp.bfloat16)
        for j in range(WIN):
            target[j, at : at + tokens, :] = turned[j * tokens : (j + 1) * tokens]

    def merge_rows(attended):
        merged = jnp.dot(attended[0], merge[0], preferred_element_type=jnp.float32)
        for j in range(1, WIN):
            merged += jnp.dot(attended[j], merge[j], preferred_element_type=jnp.float32)
        return merged

    def scaled_heads(mixed, scale):
        return jnp.concatenate(
            [mixed[h * DH : (h + 1) * DH] * scale[h : h + 1] for h in range(heads)], axis=0
        )

    for part in range(1, parts - 1):
        turn(local_mixed[part], attended_mid, (part - 1) * tokens)
    for fetch in fetches[:WIN]:
        fetch.wait()
    mid_part[...] = merge_rows(attended_mid)
    mid_move = across(0, mid_part, mid_swap)
    mid_move.start()
    units = []
    for side in range(2):
        landed(query_moves, side)
        keys_at = side * (row_len - sent)
        code = code_of(first_id if side == 0 else last_id, CODE).astype(jnp.float32)
        code = jnp.broadcast_to(code, (PACK, sent)).astype(jnp.bfloat16)
        units += [
            (
                head,
                lambda a, b, side=side: query_in[side, a:b, :],
                code,
                lambda head, at=keys_at: spread_keys[head, at : at + sent, :],
                lambda head, at=keys_at: spread_values[head, :, at : at + sent],
            )
            for head in range(heads)
        ]
    pieces, tops = soft_heads(units, 8)
    for side in range(2):
        stats = jnp.concatenate(tops[side * heads : (side + 1) * heads], axis=0)
        if side == 1:
            stats = jnp.where(link_open, stats, NEG)
        far_mixed[side] = jnp.concatenate(pieces[side * heads : (side + 1) * heads], axis=0)
        far_stats[side] = stats
        back_out[side] = stats
        begin(back_moves, side)
    for side in range(2):
        landed(stats_moves, side)
        share = 1.0 / (1.0 + jnp.exp2(stats_in[side] - far_stats[side]))
        turn(scaled_heads(far_mixed[side], share), attended_far, side * tokens)
    far_merged = merge_rows(attended_far)
    half = tokens // 2
    for side in range(2):
        for part in range(2):
            piece = far_merged[side * tokens + part * half : side * tokens + (part + 1) * half]
            far_part[part, side] = piece
            far_low[part, side] = piece.astype(jnp.bfloat16)
    far_move = across(1, far_low.at[beside], far_swap)
    far_move.start()
    far_move.wait_recv()
    for side in range(2):
        part_out[side] = (far_part[core, side] + far_swap[side].astype(jnp.float32)).astype(jnp.bfloat16)
        begin(part_moves, side)

    for side in range(2):
        landed(back_moves, side)
        back = jnp.where(inside[side], back_in[side], NEG)
        place_at = side * (parts - 1)
        share = 1.0 / (1.0 + jnp.exp2(back - local_stats[place_at]))
        turn(scaled_heads(local_mixed[place_at], share), attended_edge, side * tokens)
    edge_merged = merge_rows(attended_edge)
    for side in range(2):
        for part in range(2):
            at = side * tokens + part * half
            edge_part[part, side] = edge_merged[at : at + half]

    edge_move = across(2, edge_part, edge_swap)
    edge_move.start()

    def norm(merged):
        mean = jnp.sum(merged, axis=1, keepdims=True) / model_width
        variance = jnp.sum(merged * merged, axis=1, keepdims=True) / model_width - mean * mean
        value = (merged - mean) * lax.rsqrt(variance + EPS) * gain + bias
        return value.astype(jnp.bfloat16)

    mid_move.wait_recv()
    normed[tokens : (parts - 1) * tokens, :] = norm(mid_part[...] + mid_swap[...])

    blocks, merged_rows = groups, packed.shape[0]
    same = lax.broadcasted_iota(jnp.int32, (blocks, blocks), 0)
    same = same == lax.broadcasted_iota(jnp.int32, (blocks, blocks), 1)
    owner_col = jnp.sum(jnp.where(same, owner_row, 0), axis=1, keepdims=True)
    block_row = lax.broadcasted_iota(jnp.int32, (blocks, merged_rows), 0)
    block_of = lax.broadcasted_iota(jnp.int32, (blocks, merged_rows), 1) // rows
    owner_of = jnp.sum(jnp.where(block_row == block_of, owner_col, 0), axis=0, keepdims=True)
    earlier = jnp.logical_and(owner_col == owner_of, block_row < block_of)
    rank = jnp.sum(jnp.where(earlier, 1, 0), axis=0, keepdims=True)
    token = lax.broadcasted_iota(jnp.int32, (1, merged_rows), 1)
    target = jnp.where(rank == core, owner_of * rows + token % rows, -1)
    place = lax.broadcasted_iota(jnp.int32, (merged_rows, merged_rows), 0)
    place = jnp.where(place == target, 1.0, 0.0).astype(jnp.bfloat16)

    edge_move.wait_recv()
    share_moves = [across(3 + side, part_in.at[side], part_far.at[side]) for side in range(2)]
    for side in range(2):
        landed(part_moves, side)
        share_moves[side].start()
        at = pl.multiple_of(side * (parts - 1) * tokens + core * half, half)
        value = edge_part[core, side] + edge_swap[core, side] + part_in[side].astype(jnp.float32)
        normed[pl.ds(at, half), :] = norm(value)
    for side in range(2):
        share_moves[side].wait_recv()
        at = pl.multiple_of(side * (parts - 1) * tokens + beside * half, half)
        value = edge_part[beside, side] + edge_swap[beside, side] + part_far[side].astype(jnp.float32)
        normed[pl.ds(at, half), :] = norm(value)
    packed[...] = jnp.dot(place, normed[...], preferred_element_type=jnp.float32).astype(jnp.bfloat16)

    def outgoing(partner):
        return pltpu.make_async_remote_copy(
            src_ref=packed.at[pl.ds(pl.multiple_of(partner * rows, rows), rows), :],
            dst_ref=routed_ref.at[group, core],
            send_sem=send_sems.at[partner],
            recv_sem=recv_sems.at[group],
            device_id=(partner, core),
            device_id_type=MESH,
        )

    def incoming(source):
        return pltpu.make_async_remote_copy(
            src_ref=packed.at[pl.ds(0, rows), :],
            dst_ref=routed_ref.at[source, core],
            send_sem=send_sems.at[source],
            recv_sem=recv_sems.at[source],
            device_id=(source, core),
            device_id_type=MESH,
        )

    def handed(source, whose):
        return pltpu.make_async_remote_copy(
            src_ref=routed_ref.at[source, whose],
            dst_ref=routed_ref.at[source, whose],
            send_sem=over_sems.at[source],
            recv_sem=back_sems.at[source],
            device_id=(group, beside),
            device_id_type=MESH,
        )

    bulk = groups // 2
    mine = group // bulk
    for step in range(bulk):
        outgoing((1 - mine) * bulk + lax.rem(group + step, bulk)).start()
    for step in range(1, bulk):
        outgoing(mine * bulk + lax.rem(group + step, bulk)).start()
    own = pl.multiple_of(group * rows, rows)
    routed_ref[group, core] = packed[pl.ds(own, rows), :]
    handed(group, core).start()
    fetches[WIN].wait()
    span = bulk * CAP * rows

    @pl.loop(0, 2)
    def _(phase):
        half_at = lax.rem(mine + phase, 2)
        for step in range(bulk):
            source = half_at * bulk + lax.rem(group + bulk - step, bulk)

            @pl.when(source != group)
            def _():
                incoming(source).wait_recv()
                handed(source, core).start()

        for step in range(bulk):
            handed(half_at * bulk + step, beside).wait_recv()
        arrived = routed_ref[pl.ds(half_at * bulk, bulk)]
        routed_turned[...] = arrived.reshape(span, model_width).T
        projected = jnp.dot(next_weight[...], routed_turned[...], preferred_element_type=jnp.float32)
        out_ref[:, pl.ds(pl.multiple_of(half_at * span, span), span)] = projected.astype(jnp.bfloat16)

    for side in range(2):
        for moves in (query_moves, stats_moves, back_moves, part_moves):
            left(moves, side)
    for move in (mid_move, far_move, edge_move, *share_moves):
        move.wait_send()
    for step in range(groups):
        handed(step, core).wait_send()
    for step in range(1, groups):
        outgoing(lax.rem(group + step, groups)).wait_send()


def encode(qkv, merge_weight, gain, ids, next_weight, groups):
    width, row_len = qkv.shape[1:]
    model_width = merge_weight.shape[2]
    heads = width // DH
    parts = 4
    sent = row_len // parts
    tokens = sent // WIN
    merged_rows = row_len // WIN
    rows = merged_rows // groups
    slots = groups * CAP * rows
    vmem = pl.BlockSpec(memory_space=pltpu.VMEM)
    hbm = pl.BlockSpec(memory_space=pltpu.HBM)
    low, full = jnp.bfloat16, jnp.float32
    return pl.pallas_call(
        encoder_kernel,
        out_shape=jax.ShapeDtypeStruct((next_weight.shape[0], slots), low),
        in_specs=[hbm, hbm, vmem, vmem, hbm],
        out_specs=vmem,
        scratch_shapes=[
            pltpu.VMEM((groups, CAP, rows, model_width), low),
            pltpu.VMEM(next_weight.shape, low),
            pltpu.VMEM((model_width, slots // 2), low),
            pltpu.VMEM(qkv.shape, low),
            pltpu.VMEM(merge_weight.shape, low),
            pltpu.VMEM((heads, row_len, 2 * TILE), low),
            pltpu.VMEM((heads, SPAN, row_len), low),
            pltpu.VMEM((parts, width, sent), full),
            pltpu.VMEM((parts, heads, sent), full),
            pltpu.VMEM((2, width, sent), full),
            pltpu.VMEM((2, heads, sent), full),
            pltpu.VMEM((2, width, sent), low),
            pltpu.VMEM((2, heads, sent), full),
            pltpu.VMEM((2, heads, sent), full),
            pltpu.VMEM((2, heads, sent), full),
            pltpu.VMEM((2, heads, sent), full),
            pltpu.VMEM((WIN, 2 * tokens, width), low),
            pltpu.VMEM((WIN, 2 * tokens, width), low),
            pltpu.VMEM((WIN, 2 * tokens, width), low),
            pltpu.VMEM((2, 2, tokens // 2, model_width), full),
            pltpu.VMEM((2, 2, tokens // 2, model_width), low),
            pltpu.VMEM((2, tokens // 2, model_width), low),
            pltpu.VMEM((2, tokens // 2, model_width), low),
            pltpu.VMEM((2, tokens // 2, model_width), low),
            pltpu.VMEM((2 * tokens, model_width), full),
            pltpu.VMEM((2 * tokens, model_width), full),
            pltpu.VMEM((2, tokens // 2, model_width), low),
            pltpu.VMEM((2, 2, tokens // 2, model_width), full),
            pltpu.VMEM((2, 2, tokens // 2, model_width), full),
            pltpu.VMEM((merged_rows, model_width), low),
            pltpu.VMEM((merged_rows, model_width), low),
            pltpu.SemaphoreType.DMA((3,)),
            pltpu.SemaphoreType.DMA((WIN,)),
            pltpu.SemaphoreType.DMA,
            pltpu.SemaphoreType.DMA((4, 2)),
            pltpu.SemaphoreType.DMA((4, 2)),
            pltpu.SemaphoreType.DMA((5,)),
            pltpu.SemaphoreType.DMA((5,)),
            pltpu.SemaphoreType.DMA((groups,)),
            pltpu.SemaphoreType.DMA((groups,)),
            pltpu.SemaphoreType.DMA((groups,)),
            pltpu.SemaphoreType.DMA((groups,)),
        ],
        compiler_params=pltpu.CompilerParams(
            vmem_limit_bytes=51 << 20, collective_id=0, has_side_effects=True
        ),
        name="encode",
    )(qkv, merge_weight, gain, ids, next_weight)


def body(qkv, segments, links, owners, merge_weight, norm_gain, norm_bias, next_weight):
    row_len = qkv.shape[1]
    model_width = norm_gain.shape[0]
    tp_size = lax.axis_size("tp")
    turned = jnp.swapaxes(qkv, 1, 2)
    group_count = lax.axis_size("grp")
    owner_ids = owners[0, :, 0]
    block_count = owner_ids.shape[0]
    if tp_size == 2 and block_count == group_count:
        gain = jnp.concatenate([norm_gain, norm_bias])[None]
        ids = jnp.concatenate([segments[0], owner_ids, links])[None]
        projected = encode(turned, merge_weight, gain, ids, next_weight.T, group_count)
        return projected.T[None]
    seg_ids = segments[0]
    linked = links[0] > 0
    sent = row_len // 4
    last_flag = jnp.logical_and(seg_ids == seg_ids[row_len - 1], linked)[row_len - sent :]
    first_flag = (seg_ids == seg_ids[0])[:sent]

    def payload(pairs, flag):
        mark = jnp.broadcast_to(flag.astype(jnp.bfloat16)[None, None, :], (2, PACK, sent))
        return jnp.concatenate([pairs, mark], axis=1)

    prev = shifted(payload(turned[1:3, :, row_len - sent :], last_flag), "grp", 1)
    following = shifted(payload(turned[1:3, :, :sent], first_flag), "grp", -1)
    middle = run_attention(False, turned, segments, merge_weight, sent, None)
    partial_sum = run_attention(
        True, turned, segments, merge_weight, sent, (links, prev, following, middle)
    )
    merged_rows = row_len // WIN

    block_rows = merged_rows // block_count
    block_index = jnp.arange(block_count)
    earlier = block_index[:, None] > block_index[None, :]
    slot_rank = jnp.sum(
        jnp.logical_and(owner_ids[:, None] == owner_ids[None, :], earlier).astype(jnp.int32), axis=1
    )
    slots = group_count * CAP * block_rows

    target = (owner_ids * CAP + slot_rank)[:, None] * block_rows
    target = (target + jnp.arange(block_rows)[None, :]).reshape(merged_rows)
    merged = lax.psum(partial_sum, "tp")
    mean = jnp.mean(merged, axis=1, keepdims=True)
    variance = jnp.mean(merged * merged, axis=1, keepdims=True) - mean * mean
    normed = (merged - mean) * lax.rsqrt(variance + EPS) * norm_gain + norm_bias
    normed = normed.astype(jnp.bfloat16)
    placing = (jnp.arange(slots)[:, None] == target[None, :]).astype(jnp.bfloat16)
    packed = jnp.dot(placing, normed, preferred_element_type=jnp.float32).astype(jnp.bfloat16)
    packed = packed.reshape(group_count, CAP * block_rows, model_width)
    routed = lax.all_to_all(packed, "grp", split_axis=0, concat_axis=0, tiled=True)
    routed = routed.reshape(slots, model_width)
    projected = jnp.dot(routed, next_weight, preferred_element_type=jnp.float32)
    return projected.astype(jnp.bfloat16)[None]


def solution(mesh):
    placed = (
        P(None, "grp", "tp"),
        P("grp", None),
        P("grp"),
        P("grp", None, None),
        P(None, "tp", None),
        P(),
        P(),
        P(None, "tp"),
    )
    return jax.shard_map(
        body, mesh=mesh, in_specs=placed, out_specs=P("grp", None, "tp"), check_vma=False
    )
```

```python
import functools
import math

import jax
import jax.numpy as jnp
from jax import lax
from jax.experimental import pallas as pl
from jax.experimental.pallas import tpu as pltpu
from jax.sharding import PartitionSpec as P

DH = 88
WIN = 4
CAP = 2
TILE = 128
PACK = 16
EPS = 1e-05
NEG = -1e30
MESH = pl.DeviceIdType.MESH
SPAN = 96
CODE = 640.0
SCALE2 = math.log2(math.e) / math.sqrt(DH)


def shifted(block, axis, distance):
    devices = range(lax.axis_size(axis))
    route = [(i - distance, i) for i in devices if i - distance in devices]
    return lax.ppermute(block, axis, route)


def attend_heads(width, read_query, key_parts, bias_parts, value_parts, together=4):
    pieces = []
    for base in range(0, width // DH, together):
        lows = [head * DH for head in range(base, min(base + together, width // DH))]
        scores = []
        for low in lows:
            start, stop = low // TILE * TILE, min(width, -(-(low + DH) // TILE) * TILE)
            row = start + lax.broadcasted_iota(jnp.int32, (stop - start, 1), 0)
            inside = jnp.logical_and(row >= low, row < low + DH)
            query = read_query(start, stop)
            query = jnp.where(inside, query.astype(jnp.float32), 0.0).astype(jnp.bfloat16)
            scores.append(
                [jnp.dot(keys(start, stop), query, preferred_element_type=jnp.float32) for keys in key_parts]
            )
        scores = [[part * SCALE2 + bias for part, bias in zip(parts, bias_parts)] for parts in scores]
        tops = [
            functools.reduce(jnp.maximum, [jnp.max(part, axis=0, keepdims=True) for part in parts])
            for parts in scores
        ]
        weights = [[jnp.exp2(part - top) for part in parts] for parts, top in zip(scores, tops)]
        scales = [
            1.0 / functools.reduce(jnp.add, [jnp.sum(part, axis=0, keepdims=True) for part in parts])
            for parts in weights
        ]
        weights = [
            [(part * scale).astype(jnp.bfloat16) for part in parts] for parts, scale in zip(weights, scales)
        ]
        for low, parts in zip(lows, weights):
            start, stop = low // PACK * PACK, -(-(low + DH) // PACK) * PACK
            terms = [
                jnp.dot(values(start, stop), part, preferred_element_type=jnp.float32)
                for part, values in zip(parts, value_parts)
            ]
            pieces.append(functools.reduce(jnp.add, terms)[low - start : low - start + DH])
    return jnp.concatenate(pieces, axis=0)


def attention_kernel(edge, row_len, width, sent, *refs):
    if edge:
        seg_smem, qkv_hbm, seg_row, seg_col, merge_hbm, links, prev, following, middle, out = refs[:10]
    else:
        seg_smem, qkv_hbm, seg_row, seg_col, merge_hbm, out = refs[:6]
    attended, merge_vmem, merge_sem, qkv, qkv_sem, turned_keys, turned_sides = refs[-7:]
    tiles = row_len // TILE
    edge_tiles = sent // TILE
    tokens = TILE // WIN
    fetch = pltpu.make_async_copy(merge_hbm, merge_vmem, merge_sem)
    load = pltpu.make_async_copy(qkv_hbm, qkv, qkv_sem)
    load.start()
    fetch.start()
    if edge:
        for side, source in enumerate((prev, following)):
            for at in range(0, sent, TILE):
                turned_sides[side, at : at + TILE, :] = source[0, :width, at : at + TILE].T
    load.wait()

    @pl.loop(0, tiles)
    def _(tile):
        at = pl.multiple_of(tile * TILE, TILE)
        turned_keys[pl.ds(at, TILE), :] = qkv[1, :, pl.ds(at, TILE)].T

    ordered = lax.broadcasted_iota(jnp.int32, (TILE, TILE), 0)
    ordered = (ordered % tokens) * WIN + ordered // tokens
    order = (ordered == lax.broadcasted_iota(jnp.int32, (TILE, TILE), 1)).astype(jnp.float32)
    order = order.astype(jnp.bfloat16)

    def one(tile, out_row, neighbour):
        first = seg_smem[0, tile * TILE]
        last = seg_smem[0, tile * TILE + TILE - 1]
        begin, stop = jnp.int32(0), jnp.int32(0)
        for other in range(tiles):
            begin += (seg_smem[0, other * TILE + TILE - 1] < first).astype(jnp.int32)
            stop += (seg_smem[0, other * TILE] <= last).astype(jnp.int32)
        needed = stop - begin
        query_at = pl.multiple_of(tile * TILE, TILE)
        query_ids = seg_row[pl.ds(tile, 1), :]

        def run(count):
            key_at = pl.multiple_of(jnp.minimum(begin, tiles - count) * TILE, TILE)
            key_ids = seg_col[pl.ds(key_at, count * TILE), :]
            bias_parts = [jnp.where(key_ids == query_ids, 0.0, NEG)]
            key_parts = [lambda a, b: turned_keys[pl.ds(key_at, count * TILE), a:b]]
            value_parts = [lambda a, b: qkv[2, a:b, pl.ds(key_at, count * TILE)]]
            if neighbour is not None:
                side, source, segment, open_link = neighbour
                marks = jnp.transpose(source[0, width : width + PACK, :].astype(jnp.float32))[:, :1]
                wanted = jnp.logical_and(query_ids == segment, open_link).astype(jnp.float32)
                bias_parts.append(jnp.where(marks * wanted > 0.5, 0.0, NEG))
                key_parts.append(lambda a, b: turned_sides[side, :, a:b])
                value_parts.append(lambda a, b: source[1, a:b, :])
            mixed = attend_heads(
                width,
                lambda a, b: qkv[0, a:b, pl.ds(query_at, TILE)],
                key_parts,
                bias_parts,
                value_parts,
            )
            turned = lax.dot_general(
                order,
                mixed.astype(jnp.bfloat16),
                (((1,), (1,)), ((), ())),
                preferred_element_type=jnp.float32,
            ).astype(jnp.bfloat16)
            for j in range(WIN):
                attended[j, pl.ds(out_row, tokens), :] = turned[j * tokens : (j + 1) * tokens]

        sizes = [size for size in (2, 3, 4) if size < tiles] + [tiles]
        floor = 0
        for size in sizes:
            pl.when(jnp.logical_and(needed > floor, needed <= size))(functools.partial(run, size))
            floor = size

    if edge:
        @pl.loop(0, edge_tiles)
        def _(tile):
            one(tile, pl.multiple_of(tile * tokens, tokens), (0, prev, seg_smem[0, 0], True))

        @pl.loop(0, edge_tiles)
        def _(step):
            one(
                tiles - edge_tiles + step,
                pl.multiple_of((edge_tiles + step) * tokens, tokens),
                (1, following, seg_smem[0, row_len - 1], links[0] > 0),
            )
    else:
        @pl.loop(edge_tiles, tiles - edge_tiles)
        def _(tile):
            one(tile, pl.multiple_of((tile - edge_tiles) * tokens, tokens), None)

    fetch.wait()
    merged = jnp.dot(attended[0], merge_vmem[0], preferred_element_type=jnp.float32)
    for j in range(1, WIN):
        merged += jnp.dot(attended[j], merge_vmem[j], preferred_element_type=jnp.float32)
    if edge:
        half = merged.shape[0] // 2
        out[:half, :] = merged[:half]
        out[half : half + middle.shape[0], :] = middle[...]
        out[half + middle.shape[0] :, :] = merged[half:]
    else:
        out[...] = merged


def run_attention(edge, qkv, segments, merge_weight, sent, extra):
    width, row_len = qkv.shape[1:]
    model_width = merge_weight.shape[2]
    rows = 2 * sent if edge else row_len - 2 * sent
    smem = pl.BlockSpec(memory_space=pltpu.SMEM)
    vmem = pl.BlockSpec(memory_space=pltpu.VMEM)
    operands = [
        segments,
        qkv,
        segments.reshape(row_len // TILE, TILE),
        segments.reshape(row_len, 1),
        merge_weight,
    ]
    hbm = pl.BlockSpec(memory_space=pltpu.HBM)
    specs = [smem, hbm, vmem, vmem, hbm]
    if edge:
        operands += list(extra)
        specs += [smem, vmem, vmem, vmem]
    out_rows = row_len // WIN if edge else rows // WIN
    return pl.pallas_call(
        functools.partial(attention_kernel, edge, row_len, width, sent),
        out_shape=jax.ShapeDtypeStruct((out_rows, model_width), jnp.float32),
        in_specs=specs,
        out_specs=vmem,
        scratch_shapes=[
            pltpu.VMEM((WIN, rows // WIN, width), jnp.bfloat16),
            pltpu.VMEM(merge_weight.shape, jnp.bfloat16),
            pltpu.SemaphoreType.DMA,
            pltpu.VMEM(qkv.shape, jnp.bfloat16),
            pltpu.SemaphoreType.DMA,
            pltpu.VMEM((row_len, width), jnp.bfloat16),
            pltpu.VMEM((2, sent, width), jnp.bfloat16),
        ],
        compiler_params=pltpu.CompilerParams(vmem_limit_bytes=40 << 20),
        cost_estimate=pl.CostEstimate(
            flops=rows * 512 * width * 6, bytes_accessed=qkv.size * 2, transcendentals=rows * 512 * 8
        ),
        name="edge_attention" if edge else "middle_attention",
    )(*operands)


def spread_query(query, odd, code):
    row = lax.broadcasted_iota(jnp.int32, query.shape, 0)
    inside = row >= SPAN - DH if odd else row < DH
    scaled = jnp.where(inside, query.astype(jnp.float32) * SCALE2, 0.0)
    high = scaled.astype(jnp.bfloat16)
    low = (scaled - high.astype(jnp.float32)).astype(jnp.bfloat16)
    columns = query.shape[1]
    return jnp.concatenate(
        [high, code, jnp.zeros((TILE - SPAN - PACK, columns), jnp.bfloat16)]
        + [low, jnp.zeros((TILE - SPAN, columns), jnp.bfloat16)],
        axis=0,
    )


def soft_heads(units, together):
    pieces, tops = [], []
    for base in range(0, len(units), together):
        group = units[base : base + together]
        scores = []
        for head, read_query, code, read_keys, _ in group:
            start = head * DH // PACK * PACK
            spread = spread_query(read_query(start, start + SPAN), head % 2 == 1, code)
            scores.append(jnp.dot(read_keys(head), spread, preferred_element_type=jnp.float32))
        maxima = [jnp.max(score, axis=0, keepdims=True) for score in scores]
        weights = [jnp.exp2(score - top).astype(jnp.bfloat16) for score, top in zip(scores, maxima)]
        for (head, _, _, _, read_values), top, weight in zip(group, maxima, weights):
            mixed = jnp.dot(read_values(head), weight, preferred_element_type=jnp.float32)
            if head % 2 == 1:
                total, mixed = mixed[:1], mixed[SPAN - DH :]
            else:
                total, mixed = mixed[DH : DH + 1], mixed[:DH]
            pieces.append(mixed * (1.0 / total))
            tops.append(top + jnp.log2(total))
    return pieces, tops


def encoder_kernel(
    qkv_hbm,
    merge_hbm,
    gain_ref,
    ids_ref,
    next_hbm,
    out_ref,
    routed_ref,
    next_weight,
    routed_turned,
    qkv,
    merge,
    spread_keys,
    spread_values,
    local_mixed,
    local_stats,
    far_mixed,
    far_stats,
    query_in,
    stats_out,
    stats_in,
    back_out,
    back_in,
    attended_mid,
    attended_far,
    attended_edge,
    far_part,
    far_low,
    far_swap,
    part_out,
    part_in,
    mid_part,
    mid_swap,
    part_far,
    edge_part,
    edge_swap,
    normed,
    packed,
    load_sems,
    merge_sems,
    next_sem,
    next_send,
    next_recv,
    swap_send,
    swap_recv,
    send_sems,
    recv_sems,
    over_sems,
    back_sems,
):
    group, core = lax.axis_index("grp"), lax.axis_index("tp")
    groups = lax.axis_size("grp")
    beside = 1 - core
    width, row_len = qkv.shape[1:]
    heads = width // DH
    sent = query_in.shape[2]
    parts = row_len // sent
    tokens = sent // WIN
    rows = packed.shape[0] // groups
    model_width = merge.shape[2]
    has_prev, has_next = group > 0, group < groups - 1

    barrier = pltpu.get_barrier_semaphore()
    pl.semaphore_signal(barrier, inc=1, device_id=(group, beside), device_id_type=MESH)
    for step in range(1, groups):
        partner = lax.rem(group + step, groups)
        pl.semaphore_signal(barrier, inc=1, device_id=(partner, core), device_id_type=MESH)
    loads = [pltpu.make_async_copy(qkv_hbm.at[i], qkv.at[i], load_sems.at[i]) for i in range(3)]
    loads[1].start()
    loads[0].start()
    loads[2].start()
    fetches = [
        pltpu.make_async_copy(merge_hbm.at[j], merge.at[j], merge_sems.at[j]) for j in range(WIN)
    ]
    fetches.append(pltpu.make_async_copy(next_hbm, next_weight, next_sem))

    def along(kind, side, source, target, *where):
        partner = lax.rem(group + groups - 1, groups) if side == 0 else lax.rem(group + 1, groups)
        return pltpu.make_async_remote_copy(
            src_ref=source,
            dst_ref=target.at[(1 - side, *where)],
            send_sem=next_send.at[kind, side],
            recv_sem=next_recv.at[kind, 1 - side],
            device_id=(partner, core),
            device_id_type=MESH,
        )

    def across(kind, source, target):
        return pltpu.make_async_remote_copy(
            src_ref=source,
            dst_ref=target,
            send_sem=swap_send.at[kind],
            recv_sem=swap_recv.at[kind],
            device_id=(group, beside),
            device_id_type=MESH,
        )

    cut = heads // 2 * DH
    spans = [(0, slice(0, cut)), (4, slice(cut, width))]
    query_moves = [
        [
            along(
                kind,
                side,
                qkv_hbm.at[0, where, pl.ds(side * (row_len - sent), sent)],
                query_in,
                where,
            )
            for side in range(2)
        ]
        for kind, where in spans
    ]
    stats_moves = [along(1, side, stats_out.at[side], stats_in) for side in range(2)]
    back_moves = [along(2, side, back_out.at[side], back_in) for side in range(2)]
    part_moves = [along(3, side, part_out.at[side], part_in) for side in range(2)]
    exists = [has_prev, has_next]

    def begin(moves, side):
        pl.when(exists[side])(lambda: moves[side].start())

    def landed(moves, slot):
        pl.when(exists[slot])(lambda: moves[1 - slot].wait_recv())

    def left(moves, side):
        pl.when(exists[side])(lambda: moves[side].wait_send())

    for slot in range(2):
        @pl.when(jnp.logical_not(exists[slot]))
        def _():
            query_in[slot] = jnp.zeros(query_in.shape[1:], query_in.dtype)
            stats_in[slot] = jnp.full(stats_in.shape[1:], -NEG, jnp.float32)
            back_in[slot] = jnp.full(back_in.shape[1:], NEG, jnp.float32)
            part_in[slot] = jnp.zeros(part_in.shape[1:], part_in.dtype)

    gain, bias = gain_ref[:, :model_width], gain_ref[:, model_width:]
    ids_at = 0

    def small_ids(where):
        return ids_ref[:, where]

    seg = small_ids(slice(ids_at, ids_at + row_len))
    owners_at = ids_at + row_len
    owner_row = small_ids(slice(owners_at, owners_at + groups))
    link = ids_ref[:, owners_at + groups : owners_at + groups + 1]
    bit = jnp.left_shift(1, lax.broadcasted_iota(jnp.int32, (PACK, 1), 0))
    real = lax.broadcasted_iota(jnp.int32, (PACK, 1), 0) < 8

    def code_of(ids, size):
        sign = jnp.where(jnp.bitwise_and(ids, bit) != 0, size, -size)
        return jnp.where(real, sign, 0.0).astype(jnp.bfloat16)

    pl.semaphore_wait(barrier, groups)
    for moves in query_moves:
        begin(moves, 0)
        begin(moves, 1)
    for fetch in fetches:
        fetch.start()

    key_code = code_of(seg, 1.0)
    key_fill = jnp.zeros((TILE - SPAN - PACK, row_len), jnp.bfloat16)
    loads[1].wait()
    for head in range(heads):
        start = head * DH // PACK * PACK
        block = jnp.concatenate([qkv[1, start : start + SPAN, :], key_code, key_fill], axis=0).T
        spread_keys[head, :, :TILE] = block
        spread_keys[head, :, TILE:] = block
    loads[2].wait()
    span_row = lax.broadcasted_iota(jnp.int32, (SPAN, 1), 0)
    for head in range(heads):
        start = head * DH // PACK * PACK
        spare = span_row < SPAN - DH if head % 2 == 1 else span_row >= DH
        value = qkv[2, start : start + SPAN, :].astype(jnp.float32)
        spread_values[head] = jnp.where(spare, 1.0, value).astype(jnp.bfloat16)
    loads[0].wait()

    @pl.loop(0, parts)
    def _(part):
        at = pl.multiple_of(part * sent, sent)
        code = code_of(small_ids(pl.ds(pl.multiple_of(ids_at + at, TILE), sent)), CODE)
        units = [
            (
                head,
                lambda a, b: qkv[0, a:b, pl.ds(at, sent)],
                code,
                lambda head: spread_keys[head],
                lambda head: spread_values[head],
            )
            for head in range(heads)
        ]
        pieces, tops = soft_heads(units, 8)
        local_mixed[part] = jnp.concatenate(pieces, axis=0)
        local_stats[part] = jnp.concatenate(tops, axis=0)

    first_id, last_id = seg[:, :1], seg[:, row_len - 1 :]
    link_open = jnp.logical_and(link > 0, has_next)
    in_first = seg[:, :sent] == first_id
    in_last = jnp.logical_and(seg[:, row_len - sent :] == last_id, link_open)
    inside = [in_first, in_last]
    stats_out[0] = jnp.where(in_first, local_stats[0], -NEG)
    stats_out[1] = jnp.where(in_last, local_stats[parts - 1], -NEG)
    begin(stats_moves, 0)
    begin(stats_moves, 1)

    ordered = lax.broadcasted_iota(jnp.int32, (sent, sent), 0)
    ordered = (ordered % tokens) * WIN + ordered // tokens
    order = (ordered == lax.broadcasted_iota(jnp.int32, (sent, sent), 1)).astype(jnp.float32)
    order = order.astype(jnp.bfloat16)

    def turn(mixed, target, at):
        turned = lax.dot_general(
            order,
            mixed.astype(jnp.bfloat16),
            (((1,), (1,)), ((), ())),
            preferred_element_type=jnp.float32,
        ).astype(jnp.bfloat16)
        for j in range(WIN):
            target[j, at : at + tokens, :] = turned[j * tokens : (j + 1) * tokens]

    def merge_rows(attended):
        merged = jnp.dot(attended[0], merge[0], preferred_element_type=jnp.float32)
        for j in range(1, WIN):
            merged += jnp.dot(attended[j], merge[j], preferred_element_type=jnp.float32)
        return merged

    def scaled_heads(mixed, scale):
        return jnp.concatenate(
            [mixed[h * DH : (h + 1) * DH] * scale[h : h + 1] for h in range(heads)], axis=0
        )

    for part in range(1, parts - 1):
        turn(local_mixed[part], attended_mid, (part - 1) * tokens)
    for fetch in fetches[:WIN]:
        fetch.wait()
    mid_part[...] = merge_rows(attended_mid)
    mid_move = across(0, mid_part, mid_swap)
    mid_move.start()
    codes = []
    for own_id in (first_id, last_id):
        code = code_of(own_id, CODE).astype(jnp.float32)
        codes.append(jnp.broadcast_to(code, (PACK, sent)).astype(jnp.bfloat16))
    pieces, tops = [[], []], [[], []]
    for step, moves in enumerate(query_moves):
        units = []
        for side in range(2):
            landed(moves, side)
            keys_at = side * (row_len - sent)
            units += [
                (
                    head,
                    lambda a, b, side=side: query_in[side, a:b, :],
                    codes[side],
                    lambda head, at=keys_at: spread_keys[head, at : at + sent, :],
                    lambda head, at=keys_at: spread_values[head, :, at : at + sent],
                )
                for head in range(step * (heads // 2), heads - (1 - step) * (heads - heads // 2))
            ]
        some, highs = soft_heads(units, 8)
        half_units = len(units) // 2
        for side in range(2):
            pieces[side] += some[side * half_units : (side + 1) * half_units]
            tops[side] += highs[side * half_units : (side + 1) * half_units]
    for side in range(2):
        stats = jnp.concatenate(tops[side], axis=0)
        if side == 1:
            stats = jnp.where(link_open, stats, NEG)
        far_mixed[side] = jnp.concatenate(pieces[side], axis=0)
        far_stats[side] = stats
        back_out[side] = stats
        begin(back_moves, side)
    for side in range(2):
        landed(stats_moves, side)
        share = 1.0 / (1.0 + jnp.exp2(stats_in[side] - far_stats[side]))
        turn(scaled_heads(far_mixed[side], share), attended_far, side * tokens)
    far_merged = merge_rows(attended_far)
    half = tokens // 2
    for side in range(2):
        for part in range(2):
            piece = far_merged[side * tokens + part * half : side * tokens + (part + 1) * half]
            far_part[part, side] = piece
            far_low[part, side] = piece.astype(jnp.bfloat16)
    far_move = across(1, far_low.at[beside], far_swap)
    far_move.start()
    far_move.wait_recv()
    for side in range(2):
        part_out[side] = (far_part[core, side] + far_swap[side].astype(jnp.float32)).astype(jnp.bfloat16)
        begin(part_moves, side)

    for side in range(2):
        landed(back_moves, side)
        back = jnp.where(inside[side], back_in[side], NEG)
        place_at = side * (parts - 1)
        share = 1.0 / (1.0 + jnp.exp2(back - local_stats[place_at]))
        turn(scaled_heads(local_mixed[place_at], share), attended_edge, side * tokens)
    edge_merged = merge_rows(attended_edge)
    for side in range(2):
        for part in range(2):
            at = side * tokens + part * half
            edge_part[part, side] = edge_merged[at : at + half]

    edge_move = across(2, edge_part, edge_swap)
    edge_move.start()

    def norm(merged):
        mean = jnp.sum(merged, axis=1, keepdims=True) / model_width
        variance = jnp.sum(merged * merged, axis=1, keepdims=True) / model_width - mean * mean
        value = (merged - mean) * lax.rsqrt(variance + EPS) * gain + bias
        return value.astype(jnp.bfloat16)

    mid_move.wait_recv()
    normed[tokens : (parts - 1) * tokens, :] = norm(mid_part[...] + mid_swap[...])

    blocks, merged_rows = groups, packed.shape[0]
    same = lax.broadcasted_iota(jnp.int32, (blocks, blocks), 0)
    same = same == lax.broadcasted_iota(jnp.int32, (blocks, blocks), 1)
    owner_col = jnp.sum(jnp.where(same, owner_row, 0), axis=1, keepdims=True)
    block_row = lax.broadcasted_iota(jnp.int32, (blocks, merged_rows), 0)
    block_of = lax.broadcasted_iota(jnp.int32, (blocks, merged_rows), 1) // rows
    owner_of = jnp.sum(jnp.where(block_row == block_of, owner_col, 0), axis=0, keepdims=True)
    earlier = jnp.logical_and(owner_col == owner_of, block_row < block_of)
    rank = jnp.sum(jnp.where(earlier, 1, 0), axis=0, keepdims=True)
    token = lax.broadcasted_iota(jnp.int32, (1, merged_rows), 1)
    target = jnp.where(rank == core, owner_of * rows + token % rows, -1)
    place = lax.broadcasted_iota(jnp.int32, (merged_rows, merged_rows), 0)
    place = jnp.where(place == target, 1.0, 0.0).astype(jnp.bfloat16)

    edge_move.wait_recv()
    share_moves = [across(3 + side, part_in.at[side], part_far.at[side]) for side in range(2)]
    for side in range(2):
        landed(part_moves, side)
        share_moves[side].start()
        at = pl.multiple_of(side * (parts - 1) * tokens + core * half, half)
        value = edge_part[core, side] + edge_swap[core, side] + part_in[side].astype(jnp.float32)
        normed[pl.ds(at, half), :] = norm(value)
    for side in range(2):
        share_moves[side].wait_recv()
        at = pl.multiple_of(side * (parts - 1) * tokens + beside * half, half)
        value = edge_part[beside, side] + edge_swap[beside, side] + part_far[side].astype(jnp.float32)
        normed[pl.ds(at, half), :] = norm(value)
    packed[...] = jnp.dot(place, normed[...], preferred_element_type=jnp.float32).astype(jnp.bfloat16)

    def outgoing(partner):
        return pltpu.make_async_remote_copy(
            src_ref=packed.at[pl.ds(pl.multiple_of(partner * rows, rows), rows), :],
            dst_ref=routed_ref.at[group, core],
            send_sem=send_sems.at[partner],
            recv_sem=recv_sems.at[group],
            device_id=(partner, core),
            device_id_type=MESH,
        )

    def incoming(source):
        return pltpu.make_async_remote_copy(
            src_ref=packed.at[pl.ds(0, rows), :],
            dst_ref=routed_ref.at[source, core],
            send_sem=send_sems.at[source],
            recv_sem=recv_sems.at[source],
            device_id=(source, core),
            device_id_type=MESH,
        )

    def handed(source, whose):
        return pltpu.make_async_remote_copy(
            src_ref=routed_ref.at[source, whose],
            dst_ref=routed_ref.at[source, whose],
            send_sem=over_sems.at[source],
            recv_sem=back_sems.at[source],
            device_id=(group, beside),
            device_id_type=MESH,
        )

    bulk = groups // 2
    mine = group // bulk
    for step in range(bulk):
        outgoing((1 - mine) * bulk + lax.rem(group + step, bulk)).start()
    for step in range(1, bulk):
        outgoing(mine * bulk + lax.rem(group + step, bulk)).start()
    own = pl.multiple_of(group * rows, rows)
    routed_ref[group, core] = packed[pl.ds(own, rows), :]
    handed(group, core).start()
    fetches[WIN].wait()
    span = bulk * CAP * rows

    @pl.loop(0, 2)
    def _(phase):
        half_at = lax.rem(mine + phase, 2)
        for step in range(bulk):
            source = half_at * bulk + lax.rem(group + bulk - step, bulk)

            @pl.when(source != group)
            def _():
                incoming(source).wait_recv()
                handed(source, core).start()

        for step in range(bulk):
            handed(half_at * bulk + step, beside).wait_recv()
        arrived = routed_ref[pl.ds(half_at * bulk, bulk)]
        routed_turned[...] = arrived.reshape(span, model_width).T
        projected = jnp.dot(next_weight[...], routed_turned[...], preferred_element_type=jnp.float32)
        out_ref[:, pl.ds(pl.multiple_of(half_at * span, span), span)] = projected.astype(jnp.bfloat16)

    for side in range(2):
        for moves in (*query_moves, stats_moves, back_moves, part_moves):
            left(moves, side)
    for move in (mid_move, far_move, edge_move, *share_moves):
        move.wait_send()
    for step in range(groups):
        handed(step, core).wait_send()
    for step in range(1, groups):
        outgoing(lax.rem(group + step, groups)).wait_send()


def encode(qkv, merge_weight, gain, ids, next_weight, groups):
    width, row_len = qkv.shape[1:]
    model_width = merge_weight.shape[2]
    heads = width // DH
    parts = 4
    sent = row_len // parts
    tokens = sent // WIN
    merged_rows = row_len // WIN
    rows = merged_rows // groups
    slots = groups * CAP * rows
    vmem = pl.BlockSpec(memory_space=pltpu.VMEM)
    hbm = pl.BlockSpec(memory_space=pltpu.HBM)
    low, full = jnp.bfloat16, jnp.float32
    return pl.pallas_call(
        encoder_kernel,
        out_shape=jax.ShapeDtypeStruct((next_weight.shape[0], slots), low),
        in_specs=[hbm, hbm, vmem, vmem, hbm],
        out_specs=vmem,
        scratch_shapes=[
            pltpu.VMEM((groups, CAP, rows, model_width), low),
            pltpu.VMEM(next_weight.shape, low),
            pltpu.VMEM((model_width, slots // 2), low),
            pltpu.VMEM(qkv.shape, low),
            pltpu.VMEM(merge_weight.shape, low),
            pltpu.VMEM((heads, row_len, 2 * TILE), low),
            pltpu.VMEM((heads, SPAN, row_len), low),
            pltpu.VMEM((parts, width, sent), full),
            pltpu.VMEM((parts, heads, sent), full),
            pltpu.VMEM((2, width, sent), full),
            pltpu.VMEM((2, heads, sent), full),
            pltpu.VMEM((2, width, sent), low),
            pltpu.VMEM((2, heads, sent), full),
            pltpu.VMEM((2, heads, sent), full),
            pltpu.VMEM((2, heads, sent), full),
            pltpu.VMEM((2, heads, sent), full),
            pltpu.VMEM((WIN, 2 * tokens, width), low),
            pltpu.VMEM((WIN, 2 * tokens, width), low),
            pltpu.VMEM((WIN, 2 * tokens, width), low),
            pltpu.VMEM((2, 2, tokens // 2, model_width), full),
            pltpu.VMEM((2, 2, tokens // 2, model_width), low),
            pltpu.VMEM((2, tokens // 2, model_width), low),
            pltpu.VMEM((2, tokens // 2, model_width), low),
            pltpu.VMEM((2, tokens // 2, model_width), low),
            pltpu.VMEM((2 * tokens, model_width), full),
            pltpu.VMEM((2 * tokens, model_width), full),
            pltpu.VMEM((2, tokens // 2, model_width), low),
            pltpu.VMEM((2, 2, tokens // 2, model_width), full),
            pltpu.VMEM((2, 2, tokens // 2, model_width), full),
            pltpu.VMEM((merged_rows, model_width), low),
            pltpu.VMEM((merged_rows, model_width), low),
            pltpu.SemaphoreType.DMA((3,)),
            pltpu.SemaphoreType.DMA((WIN,)),
            pltpu.SemaphoreType.DMA,
            pltpu.SemaphoreType.DMA((5, 2)),
            pltpu.SemaphoreType.DMA((5, 2)),
            pltpu.SemaphoreType.DMA((5,)),
            pltpu.SemaphoreType.DMA((5,)),
            pltpu.SemaphoreType.DMA((groups,)),
            pltpu.SemaphoreType.DMA((groups,)),
            pltpu.SemaphoreType.DMA((groups,)),
            pltpu.SemaphoreType.DMA((groups,)),
        ],
        compiler_params=pltpu.CompilerParams(
            vmem_limit_bytes=51 << 20, collective_id=0, has_side_effects=True
        ),
        name="encode",
    )(qkv, merge_weight, gain, ids, next_weight)


def body(qkv, segments, links, owners, merge_weight, norm_gain, norm_bias, next_weight):
    row_len = qkv.shape[1]
    model_width = norm_gain.shape[0]
    tp_size = lax.axis_size("tp")
    turned = jnp.swapaxes(qkv, 1, 2)
    group_count = lax.axis_size("grp")
    owner_ids = owners[0, :, 0]
    block_count = owner_ids.shape[0]
    if tp_size == 2 and block_count == group_count:
        gain = jnp.concatenate([norm_gain, norm_bias])[None]
        ids = jnp.concatenate([segments[0], owner_ids, links])[None]
        projected = encode(turned, merge_weight, gain, ids, next_weight.T, group_count)
        return projected.T[None]
    seg_ids = segments[0]
    linked = links[0] > 0
    sent = row_len // 4
    last_flag = jnp.logical_and(seg_ids == seg_ids[row_len - 1], linked)[row_len - sent :]
    first_flag = (seg_ids == seg_ids[0])[:sent]

    def payload(pairs, flag):
        mark = jnp.broadcast_to(flag.astype(jnp.bfloat16)[None, None, :], (2, PACK, sent))
        return jnp.concatenate([pairs, mark], axis=1)

    prev = shifted(payload(turned[1:3, :, row_len - sent :], last_flag), "grp", 1)
    following = shifted(payload(turned[1:3, :, :sent], first_flag), "grp", -1)
    middle = run_attention(False, turned, segments, merge_weight, sent, None)
    partial_sum = run_attention(
        True, turned, segments, merge_weight, sent, (links, prev, following, middle)
    )
    merged_rows = row_len // WIN

    block_rows = merged_rows // block_count
    block_index = jnp.arange(block_count)
    earlier = block_index[:, None] > block_index[None, :]
    slot_rank = jnp.sum(
        jnp.logical_and(owner_ids[:, None] == owner_ids[None, :], earlier).astype(jnp.int32), axis=1
    )
    slots = group_count * CAP * block_rows

    target = (owner_ids * CAP + slot_rank)[:, None] * block_rows
    target = (target + jnp.arange(block_rows)[None, :]).reshape(merged_rows)
    merged = lax.psum(partial_sum, "tp")
    mean = jnp.mean(merged, axis=1, keepdims=True)
    variance = jnp.mean(merged * merged, axis=1, keepdims=True) - mean * mean
    normed = (merged - mean) * lax.rsqrt(variance + EPS) * norm_gain + norm_bias
    normed = normed.astype(jnp.bfloat16)
    placing = (jnp.arange(slots)[:, None] == target[None, :]).astype(jnp.bfloat16)
    packed = jnp.dot(placing, normed, preferred_element_type=jnp.float32).astype(jnp.bfloat16)
    packed = packed.reshape(group_count, CAP * block_rows, model_width)
    routed = lax.all_to_all(packed, "grp", split_axis=0, concat_axis=0, tiled=True)
    routed = routed.reshape(slots, model_width)
    projected = jnp.dot(routed, next_weight, preferred_element_type=jnp.float32)
    return projected.astype(jnp.bfloat16)[None]


def solution(mesh):
    placed = (
        P(None, "grp", "tp"),
        P("grp", None),
        P("grp"),
        P("grp", None, None),
        P(None, "tp", None),
        P(),
        P(),
        P(None, "tp"),
    )
    return jax.shard_map(
        body, mesh=mesh, in_specs=placed, out_specs=P("grp", None, "tp"), check_vma=False
    )
```

```python
import functools
import math

import jax
import jax.numpy as jnp
from jax import lax
from jax.experimental import pallas as pl
from jax.experimental.pallas import tpu as pltpu
from jax.sharding import PartitionSpec as P

DH = 88
WIN = 4
CAP = 2
TILE = 128
PACK = 16
EPS = 1e-05
NEG = -1e30
MESH = pl.DeviceIdType.MESH
SPAN = 96
CODE = 640.0
SCALE2 = math.log2(math.e) / math.sqrt(DH)


def shifted(block, axis, distance):
    devices = range(lax.axis_size(axis))
    route = [(i - distance, i) for i in devices if i - distance in devices]
    return lax.ppermute(block, axis, route)


def attend_heads(width, read_query, key_parts, bias_parts, value_parts, together=4):
    pieces = []
    for base in range(0, width // DH, together):
        lows = [head * DH for head in range(base, min(base + together, width // DH))]
        scores = []
        for low in lows:
            start, stop = low // TILE * TILE, min(width, -(-(low + DH) // TILE) * TILE)
            row = start + lax.broadcasted_iota(jnp.int32, (stop - start, 1), 0)
            inside = jnp.logical_and(row >= low, row < low + DH)
            query = read_query(start, stop)
            query = jnp.where(inside, query.astype(jnp.float32), 0.0).astype(jnp.bfloat16)
            scores.append(
                [jnp.dot(keys(start, stop), query, preferred_element_type=jnp.float32) for keys in key_parts]
            )
        scores = [[part * SCALE2 + bias for part, bias in zip(parts, bias_parts)] for parts in scores]
        tops = [
            functools.reduce(jnp.maximum, [jnp.max(part, axis=0, keepdims=True) for part in parts])
            for parts in scores
        ]
        weights = [[jnp.exp2(part - top) for part in parts] for parts, top in zip(scores, tops)]
        scales = [
            1.0 / functools.reduce(jnp.add, [jnp.sum(part, axis=0, keepdims=True) for part in parts])
            for parts in weights
        ]
        weights = [
            [(part * scale).astype(jnp.bfloat16) for part in parts] for parts, scale in zip(weights, scales)
        ]
        for low, parts in zip(lows, weights):
            start, stop = low // PACK * PACK, -(-(low + DH) // PACK) * PACK
            terms = [
                jnp.dot(values(start, stop), part, preferred_element_type=jnp.float32)
                for part, values in zip(parts, value_parts)
            ]
            pieces.append(functools.reduce(jnp.add, terms)[low - start : low - start + DH])
    return jnp.concatenate(pieces, axis=0)


def attention_kernel(edge, row_len, width, sent, *refs):
    if edge:
        seg_smem, qkv_hbm, seg_row, seg_col, merge_hbm, links, prev, following, middle, out = refs[:10]
    else:
        seg_smem, qkv_hbm, seg_row, seg_col, merge_hbm, out = refs[:6]
    attended, merge_vmem, merge_sem, qkv, qkv_sem, turned_keys, turned_sides = refs[-7:]
    tiles = row_len // TILE
    edge_tiles = sent // TILE
    tokens = TILE // WIN
    fetch = pltpu.make_async_copy(merge_hbm, merge_vmem, merge_sem)
    load = pltpu.make_async_copy(qkv_hbm, qkv, qkv_sem)
    load.start()
    fetch.start()
    if edge:
        for side, source in enumerate((prev, following)):
            for at in range(0, sent, TILE):
                turned_sides[side, at : at + TILE, :] = source[0, :width, at : at + TILE].T
    load.wait()

    @pl.loop(0, tiles)
    def _(tile):
        at = pl.multiple_of(tile * TILE, TILE)
        turned_keys[pl.ds(at, TILE), :] = qkv[1, :, pl.ds(at, TILE)].T

    ordered = lax.broadcasted_iota(jnp.int32, (TILE, TILE), 0)
    ordered = (ordered % tokens) * WIN + ordered // tokens
    order = (ordered == lax.broadcasted_iota(jnp.int32, (TILE, TILE), 1)).astype(jnp.float32)
    order = order.astype(jnp.bfloat16)

    def one(tile, out_row, neighbour):
        first = seg_smem[0, tile * TILE]
        last = seg_smem[0, tile * TILE + TILE - 1]
        begin, stop = jnp.int32(0), jnp.int32(0)
        for other in range(tiles):
            begin += (seg_smem[0, other * TILE + TILE - 1] < first).astype(jnp.int32)
            stop += (seg_smem[0, other * TILE] <= last).astype(jnp.int32)
        needed = stop - begin
        query_at = pl.multiple_of(tile * TILE, TILE)
        query_ids = seg_row[pl.ds(tile, 1), :]

        def run(count):
            key_at = pl.multiple_of(jnp.minimum(begin, tiles - count) * TILE, TILE)
            key_ids = seg_col[pl.ds(key_at, count * TILE), :]
            bias_parts = [jnp.where(key_ids == query_ids, 0.0, NEG)]
            key_parts = [lambda a, b: turned_keys[pl.ds(key_at, count * TILE), a:b]]
            value_parts = [lambda a, b: qkv[2, a:b, pl.ds(key_at, count * TILE)]]
            if neighbour is not None:
                side, source, segment, open_link = neighbour
                marks = jnp.transpose(source[0, width : width + PACK, :].astype(jnp.float32))[:, :1]
                wanted = jnp.logical_and(query_ids == segment, open_link).astype(jnp.float32)
                bias_parts.append(jnp.where(marks * wanted > 0.5, 0.0, NEG))
                key_parts.append(lambda a, b: turned_sides[side, :, a:b])
                value_parts.append(lambda a, b: source[1, a:b, :])
            mixed = attend_heads(
                width,
                lambda a, b: qkv[0, a:b, pl.ds(query_at, TILE)],
                key_parts,
                bias_parts,
                value_parts,
            )
            turned = lax.dot_general(
                order,
                mixed.astype(jnp.bfloat16),
                (((1,), (1,)), ((), ())),
                preferred_element_type=jnp.float32,
            ).astype(jnp.bfloat16)
            for j in range(WIN):
                attended[j, pl.ds(out_row, tokens), :] = turned[j * tokens : (j + 1) * tokens]

        sizes = [size for size in (2, 3, 4) if size < tiles] + [tiles]
        floor = 0
        for size in sizes:
            pl.when(jnp.logical_and(needed > floor, needed <= size))(functools.partial(run, size))
            floor = size

    if edge:
        @pl.loop(0, edge_tiles)
        def _(tile):
            one(tile, pl.multiple_of(tile * tokens, tokens), (0, prev, seg_smem[0, 0], True))

        @pl.loop(0, edge_tiles)
        def _(step):
            one(
                tiles - edge_tiles + step,
                pl.multiple_of((edge_tiles + step) * tokens, tokens),
                (1, following, seg_smem[0, row_len - 1], links[0] > 0),
            )
    else:
        @pl.loop(edge_tiles, tiles - edge_tiles)
        def _(tile):
            one(tile, pl.multiple_of((tile - edge_tiles) * tokens, tokens), None)

    fetch.wait()
    merged = jnp.dot(attended[0], merge_vmem[0], preferred_element_type=jnp.float32)
    for j in range(1, WIN):
        merged += jnp.dot(attended[j], merge_vmem[j], preferred_element_type=jnp.float32)
    if edge:
        half = merged.shape[0] // 2
        out[:half, :] = merged[:half]
        out[half : half + middle.shape[0], :] = middle[...]
        out[half + middle.shape[0] :, :] = merged[half:]
    else:
        out[...] = merged


def run_attention(edge, qkv, segments, merge_weight, sent, extra):
    width, row_len = qkv.shape[1:]
    model_width = merge_weight.shape[2]
    rows = 2 * sent if edge else row_len - 2 * sent
    smem = pl.BlockSpec(memory_space=pltpu.SMEM)
    vmem = pl.BlockSpec(memory_space=pltpu.VMEM)
    operands = [
        segments,
        qkv,
        segments.reshape(row_len // TILE, TILE),
        segments.reshape(row_len, 1),
        merge_weight,
    ]
    hbm = pl.BlockSpec(memory_space=pltpu.HBM)
    specs = [smem, hbm, vmem, vmem, hbm]
    if edge:
        operands += list(extra)
        specs += [smem, vmem, vmem, vmem]
    out_rows = row_len // WIN if edge else rows // WIN
    return pl.pallas_call(
        functools.partial(attention_kernel, edge, row_len, width, sent),
        out_shape=jax.ShapeDtypeStruct((out_rows, model_width), jnp.float32),
        in_specs=specs,
        out_specs=vmem,
        scratch_shapes=[
            pltpu.VMEM((WIN, rows // WIN, width), jnp.bfloat16),
            pltpu.VMEM(merge_weight.shape, jnp.bfloat16),
            pltpu.SemaphoreType.DMA,
            pltpu.VMEM(qkv.shape, jnp.bfloat16),
            pltpu.SemaphoreType.DMA,
            pltpu.VMEM((row_len, width), jnp.bfloat16),
            pltpu.VMEM((2, sent, width), jnp.bfloat16),
        ],
        compiler_params=pltpu.CompilerParams(vmem_limit_bytes=40 << 20),
        cost_estimate=pl.CostEstimate(
            flops=rows * 512 * width * 6, bytes_accessed=qkv.size * 2, transcendentals=rows * 512 * 8
        ),
        name="edge_attention" if edge else "middle_attention",
    )(*operands)


def spread_query(query, odd, code):
    row = lax.broadcasted_iota(jnp.int32, query.shape, 0)
    inside = row >= SPAN - DH if odd else row < DH
    scaled = jnp.where(inside, query.astype(jnp.float32) * SCALE2, 0.0)
    high = scaled.astype(jnp.bfloat16)
    low = (scaled - high.astype(jnp.float32)).astype(jnp.bfloat16)
    columns = query.shape[1]
    return jnp.concatenate(
        [high, code, jnp.zeros((TILE - SPAN - PACK, columns), jnp.bfloat16)]
        + [low, jnp.zeros((TILE - SPAN, columns), jnp.bfloat16)],
        axis=0,
    )


def soft_heads(units, together):
    pieces, tops = [], []
    for base in range(0, len(units), together):
        group = units[base : base + together]
        scores = []
        for head, read_query, code, read_keys, _ in group:
            start = head * DH // PACK * PACK
            spread = spread_query(read_query(start, start + SPAN), head % 2 == 1, code)
            scores.append(jnp.dot(read_keys(head), spread, preferred_element_type=jnp.float32))
        maxima = [jnp.max(score, axis=0, keepdims=True) for score in scores]
        weights = [jnp.exp2(score - top).astype(jnp.bfloat16) for score, top in zip(scores, maxima)]
        for (head, _, _, _, read_values), top, weight in zip(group, maxima, weights):
            mixed = jnp.dot(read_values(head), weight, preferred_element_type=jnp.float32)
            if head % 2 == 1:
                total, mixed = mixed[:1], mixed[SPAN - DH :]
            else:
                total, mixed = mixed[DH : DH + 1], mixed[:DH]
            pieces.append(mixed * (1.0 / total))
            tops.append(top + jnp.log2(total))
    return pieces, tops


def encoder_kernel(
    qkv_hbm,
    merge_hbm,
    gain_ref,
    ids_ref,
    next_hbm,
    out_ref,
    routed_ref,
    next_weight,
    routed_turned,
    qkv,
    merge,
    spread_keys,
    spread_values,
    local_mixed,
    local_stats,
    far_mixed,
    far_stats,
    query_in,
    stats_out,
    stats_in,
    back_out,
    back_in,
    attended_mid,
    attended_far,
    attended_edge,
    far_part,
    far_low,
    far_swap,
    part_out,
    part_in,
    mid_part,
    mid_swap,
    part_far,
    edge_part,
    edge_swap,
    normed,
    packed,
    load_sems,
    merge_sems,
    next_sem,
    next_send,
    next_recv,
    swap_send,
    swap_recv,
    send_sems,
    recv_sems,
    over_sems,
    back_sems,
):
    group, core = lax.axis_index("grp"), lax.axis_index("tp")
    groups = lax.axis_size("grp")
    beside = 1 - core
    width, row_len = qkv.shape[1:]
    heads = width // DH
    sent = query_in.shape[2]
    parts = row_len // sent
    tokens = sent // WIN
    rows = packed.shape[0] // groups
    model_width = merge.shape[2]
    has_prev, has_next = group > 0, group < groups - 1

    barrier = pltpu.get_barrier_semaphore()
    pl.semaphore_signal(barrier, inc=1, device_id=(group, beside), device_id_type=MESH)
    for step in range(1, groups):
        partner = lax.rem(group + step, groups)
        pl.semaphore_signal(barrier, inc=1, device_id=(partner, core), device_id_type=MESH)
    loads = [pltpu.make_async_copy(qkv_hbm.at[i], qkv.at[i], load_sems.at[i]) for i in range(3)]
    loads[1].start()
    loads[0].start()
    loads[2].start()
    fetches = [
        pltpu.make_async_copy(merge_hbm.at[j], merge.at[j], merge_sems.at[j]) for j in range(WIN)
    ]
    fetches.append(pltpu.make_async_copy(next_hbm, next_weight, next_sem))

    def along(kind, side, source, target, *where):
        partner = lax.rem(group + groups - 1, groups) if side == 0 else lax.rem(group + 1, groups)
        return pltpu.make_async_remote_copy(
            src_ref=source,
            dst_ref=target.at[(1 - side, *where)],
            send_sem=next_send.at[kind, side],
            recv_sem=next_recv.at[kind, 1 - side],
            device_id=(partner, core),
            device_id_type=MESH,
        )

    def across(kind, source, target):
        return pltpu.make_async_remote_copy(
            src_ref=source,
            dst_ref=target,
            send_sem=swap_send.at[kind],
            recv_sem=swap_recv.at[kind],
            device_id=(group, beside),
            device_id_type=MESH,
        )

    early = heads // 4 * 3
    cut = early * DH
    spans = [(0, slice(0, cut)), (4, slice(cut, width))]
    query_moves = [
        [
            along(
                kind,
                side,
                qkv_hbm.at[0, where, pl.ds(side * (row_len - sent), sent)],
                query_in,
                where,
            )
            for side in range(2)
        ]
        for kind, where in spans
    ]
    stats_moves = [along(1, side, stats_out.at[side], stats_in) for side in range(2)]
    back_moves = [along(2, side, back_out.at[side], back_in) for side in range(2)]
    part_moves = [along(3, side, part_out.at[side], part_in) for side in range(2)]
    exists = [has_prev, has_next]

    def begin(moves, side):
        pl.when(exists[side])(lambda: moves[side].start())

    def landed(moves, slot):
        pl.when(exists[slot])(lambda: moves[1 - slot].wait_recv())

    def left(moves, side):
        pl.when(exists[side])(lambda: moves[side].wait_send())

    for slot in range(2):
        @pl.when(jnp.logical_not(exists[slot]))
        def _():
            query_in[slot] = jnp.zeros(query_in.shape[1:], query_in.dtype)
            stats_in[slot] = jnp.full(stats_in.shape[1:], -NEG, jnp.float32)
            back_in[slot] = jnp.full(back_in.shape[1:], NEG, jnp.float32)
            part_in[slot] = jnp.zeros(part_in.shape[1:], part_in.dtype)

    gain, bias = gain_ref[:, :model_width], gain_ref[:, model_width:]
    ids_at = 0

    def small_ids(where):
        return ids_ref[:, where]

    seg = small_ids(slice(ids_at, ids_at + row_len))
    owners_at = ids_at + row_len
    owner_row = small_ids(slice(owners_at, owners_at + groups))
    link = ids_ref[:, owners_at + groups : owners_at + groups + 1]
    bit = jnp.left_shift(1, lax.broadcasted_iota(jnp.int32, (PACK, 1), 0))
    real = lax.broadcasted_iota(jnp.int32, (PACK, 1), 0) < 8

    def code_of(ids, size):
        sign = jnp.where(jnp.bitwise_and(ids, bit) != 0, size, -size)
        return jnp.where(real, sign, 0.0).astype(jnp.bfloat16)

    pl.semaphore_wait(barrier, groups)
    for moves in query_moves:
        begin(moves, 0)
        begin(moves, 1)
    for fetch in fetches:
        fetch.start()

    key_code = code_of(seg, 1.0)
    key_fill = jnp.zeros((TILE - SPAN - PACK, row_len), jnp.bfloat16)
    loads[1].wait()
    for head in range(heads):
        start = head * DH // PACK * PACK
        block = jnp.concatenate([qkv[1, start : start + SPAN, :], key_code, key_fill], axis=0).T
        spread_keys[head, :, :TILE] = block
        spread_keys[head, :, TILE:] = block
    loads[2].wait()
    span_row = lax.broadcasted_iota(jnp.int32, (SPAN, 1), 0)
    for head in range(heads):
        start = head * DH // PACK * PACK
        spare = span_row < SPAN - DH if head % 2 == 1 else span_row >= DH
        value = qkv[2, start : start + SPAN, :].astype(jnp.float32)
        spread_values[head] = jnp.where(spare, 1.0, value).astype(jnp.bfloat16)
    loads[0].wait()

    @pl.loop(0, parts)
    def _(part):
        at = pl.multiple_of(part * sent, sent)
        code = code_of(small_ids(pl.ds(pl.multiple_of(ids_at + at, TILE), sent)), CODE)
        units = [
            (
                head,
                lambda a, b: qkv[0, a:b, pl.ds(at, sent)],
                code,
                lambda head: spread_keys[head],
                lambda head: spread_values[head],
            )
            for head in range(heads)
        ]
        pieces, tops = soft_heads(units, 8)
        local_mixed[part] = jnp.concatenate(pieces, axis=0)
        local_stats[part] = jnp.concatenate(tops, axis=0)

    first_id, last_id = seg[:, :1], seg[:, row_len - 1 :]
    link_open = jnp.logical_and(link > 0, has_next)
    in_first = seg[:, :sent] == first_id
    in_last = jnp.logical_and(seg[:, row_len - sent :] == last_id, link_open)
    inside = [in_first, in_last]
    stats_out[0] = jnp.where(in_first, local_stats[0], -NEG)
    stats_out[1] = jnp.where(in_last, local_stats[parts - 1], -NEG)
    begin(stats_moves, 0)
    begin(stats_moves, 1)

    ordered = lax.broadcasted_iota(jnp.int32, (sent, sent), 0)
    ordered = (ordered % tokens) * WIN + ordered // tokens
    order = (ordered == lax.broadcasted_iota(jnp.int32, (sent, sent), 1)).astype(jnp.float32)
    order = order.astype(jnp.bfloat16)

    def turn(mixed, target, at):
        turned = lax.dot_general(
            order,
            mixed.astype(jnp.bfloat16),
            (((1,), (1,)), ((), ())),
            preferred_element_type=jnp.float32,
        ).astype(jnp.bfloat16)
        for j in range(WIN):
            target[j, at : at + tokens, :] = turned[j * tokens : (j + 1) * tokens]

    def merge_rows(attended):
        merged = jnp.dot(attended[0], merge[0], preferred_element_type=jnp.float32)
        for j in range(1, WIN):
            merged += jnp.dot(attended[j], merge[j], preferred_element_type=jnp.float32)
        return merged

    def scaled_heads(mixed, scale):
        return jnp.concatenate(
            [mixed[h * DH : (h + 1) * DH] * scale[h : h + 1] for h in range(heads)], axis=0
        )

    for part in range(1, parts - 1):
        turn(local_mixed[part], attended_mid, (part - 1) * tokens)
    for fetch in fetches[:WIN]:
        fetch.wait()
    mid_part[...] = merge_rows(attended_mid)
    mid_move = across(0, mid_part, mid_swap)
    mid_move.start()
    codes = []
    for own_id in (first_id, last_id):
        code = code_of(own_id, CODE).astype(jnp.float32)
        codes.append(jnp.broadcast_to(code, (PACK, sent)).astype(jnp.bfloat16))
    pieces, tops = [[], []], [[], []]
    for step, moves in enumerate(query_moves):
        units = []
        for side in range(2):
            landed(moves, side)
            keys_at = side * (row_len - sent)
            units += [
                (
                    head,
                    lambda a, b, side=side: query_in[side, a:b, :],
                    codes[side],
                    lambda head, at=keys_at: spread_keys[head, at : at + sent, :],
                    lambda head, at=keys_at: spread_values[head, :, at : at + sent],
                )
                for head in (range(early, heads) if step else range(early))
            ]
        some, highs = soft_heads(units, 8)
        half_units = len(units) // 2
        for side in range(2):
            pieces[side] += some[side * half_units : (side + 1) * half_units]
            tops[side] += highs[side * half_units : (side + 1) * half_units]
    for side in range(2):
        stats = jnp.concatenate(tops[side], axis=0)
        if side == 1:
            stats = jnp.where(link_open, stats, NEG)
        far_mixed[side] = jnp.concatenate(pieces[side], axis=0)
        far_stats[side] = stats
        back_out[side] = stats
        begin(back_moves, side)
    for side in range(2):
        landed(stats_moves, side)
        share = 1.0 / (1.0 + jnp.exp2(stats_in[side] - far_stats[side]))
        turn(scaled_heads(far_mixed[side], share), attended_far, side * tokens)
    far_merged = merge_rows(attended_far)
    half = tokens // 2
    for side in range(2):
        for part in range(2):
            piece = far_merged[side * tokens + part * half : side * tokens + (part + 1) * half]
            far_part[part, side] = piece
            far_low[part, side] = piece.astype(jnp.bfloat16)
    far_move = across(1, far_low.at[beside], far_swap)
    far_move.start()
    far_move.wait_recv()
    for side in range(2):
        part_out[side] = (far_part[core, side] + far_swap[side].astype(jnp.float32)).astype(jnp.bfloat16)
        begin(part_moves, side)

    for side in range(2):
        landed(back_moves, side)
        back = jnp.where(inside[side], back_in[side], NEG)
        place_at = side * (parts - 1)
        share = 1.0 / (1.0 + jnp.exp2(back - local_stats[place_at]))
        turn(scaled_heads(local_mixed[place_at], share), attended_edge, side * tokens)
    edge_merged = merge_rows(attended_edge)
    for side in range(2):
        for part in range(2):
            at = side * tokens + part * half
            edge_part[part, side] = edge_merged[at : at + half]

    edge_move = across(2, edge_part, edge_swap)
    edge_move.start()

    def norm(merged):
        mean = jnp.sum(merged, axis=1, keepdims=True) / model_width
        variance = jnp.sum(merged * merged, axis=1, keepdims=True) / model_width - mean * mean
        value = (merged - mean) * lax.rsqrt(variance + EPS) * gain + bias
        return value.astype(jnp.bfloat16)

    mid_move.wait_recv()
    normed[tokens : (parts - 1) * tokens, :] = norm(mid_part[...] + mid_swap[...])

    blocks, merged_rows = groups, packed.shape[0]
    same = lax.broadcasted_iota(jnp.int32, (blocks, blocks), 0)
    same = same == lax.broadcasted_iota(jnp.int32, (blocks, blocks), 1)
    owner_col = jnp.sum(jnp.where(same, owner_row, 0), axis=1, keepdims=True)
    block_row = lax.broadcasted_iota(jnp.int32, (blocks, merged_rows), 0)
    block_of = lax.broadcasted_iota(jnp.int32, (blocks, merged_rows), 1) // rows
    owner_of = jnp.sum(jnp.where(block_row == block_of, owner_col, 0), axis=0, keepdims=True)
    earlier = jnp.logical_and(owner_col == owner_of, block_row < block_of)
    rank = jnp.sum(jnp.where(earlier, 1, 0), axis=0, keepdims=True)
    token = lax.broadcasted_iota(jnp.int32, (1, merged_rows), 1)
    target = jnp.where(rank == core, owner_of * rows + token % rows, -1)
    place = lax.broadcasted_iota(jnp.int32, (merged_rows, merged_rows), 0)
    place = jnp.where(place == target, 1.0, 0.0).astype(jnp.bfloat16)

    edge_move.wait_recv()
    share_moves = [across(3 + side, part_in.at[side], part_far.at[side]) for side in range(2)]
    for side in range(2):
        landed(part_moves, side)
        share_moves[side].start()
        at = pl.multiple_of(side * (parts - 1) * tokens + core * half, half)
        value = edge_part[core, side] + edge_swap[core, side] + part_in[side].astype(jnp.float32)
        normed[pl.ds(at, half), :] = norm(value)
    for side in range(2):
        share_moves[side].wait_recv()
        at = pl.multiple_of(side * (parts - 1) * tokens + beside * half, half)
        value = edge_part[beside, side] + edge_swap[beside, side] + part_far[side].astype(jnp.float32)
        normed[pl.ds(at, half), :] = norm(value)
    packed[...] = jnp.dot(place, normed[...], preferred_element_type=jnp.float32).astype(jnp.bfloat16)

    def outgoing(partner):
        return pltpu.make_async_remote_copy(
            src_ref=packed.at[pl.ds(pl.multiple_of(partner * rows, rows), rows), :],
            dst_ref=routed_ref.at[group, core],
            send_sem=send_sems.at[partner],
            recv_sem=recv_sems.at[group],
            device_id=(partner, core),
            device_id_type=MESH,
        )

    def incoming(source):
        return pltpu.make_async_remote_copy(
            src_ref=packed.at[pl.ds(0, rows), :],
            dst_ref=routed_ref.at[source, core],
            send_sem=send_sems.at[source],
            recv_sem=recv_sems.at[source],
            device_id=(source, core),
            device_id_type=MESH,
        )

    def handed(source, whose):
        return pltpu.make_async_remote_copy(
            src_ref=routed_ref.at[source, whose],
            dst_ref=routed_ref.at[source, whose],
            send_sem=over_sems.at[source],
            recv_sem=back_sems.at[source],
            device_id=(group, beside),
            device_id_type=MESH,
        )

    bulk = groups // 2
    mine = group // bulk
    for step in range(bulk):
        outgoing((1 - mine) * bulk + lax.rem(group + step, bulk)).start()
    for step in range(1, bulk):
        outgoing(mine * bulk + lax.rem(group + step, bulk)).start()
    own = pl.multiple_of(group * rows, rows)
    routed_ref[group, core] = packed[pl.ds(own, rows), :]
    handed(group, core).start()
    fetches[WIN].wait()
    span = bulk * CAP * rows

    @pl.loop(0, 2)
    def _(phase):
        half_at = lax.rem(mine + phase, 2)
        for step in range(bulk):
            source = half_at * bulk + lax.rem(group + bulk - step, bulk)

            @pl.when(source != group)
            def _():
                incoming(source).wait_recv()
                handed(source, core).start()

        for step in range(bulk):
            handed(half_at * bulk + step, beside).wait_recv()
        arrived = routed_ref[pl.ds(half_at * bulk, bulk)]
        routed_turned[...] = arrived.reshape(span, model_width).T
        projected = jnp.dot(next_weight[...], routed_turned[...], preferred_element_type=jnp.float32)
        out_ref[:, pl.ds(pl.multiple_of(half_at * span, span), span)] = projected.astype(jnp.bfloat16)

    for side in range(2):
        for moves in (*query_moves, stats_moves, back_moves, part_moves):
            left(moves, side)
    for move in (mid_move, far_move, edge_move, *share_moves):
        move.wait_send()
    for step in range(groups):
        handed(step, core).wait_send()
    for step in range(1, groups):
        outgoing(lax.rem(group + step, groups)).wait_send()


def encode(qkv, merge_weight, gain, ids, next_weight, groups):
    width, row_len = qkv.shape[1:]
    model_width = merge_weight.shape[2]
    heads = width // DH
    parts = 4
    sent = row_len // parts
    tokens = sent // WIN
    merged_rows = row_len // WIN
    rows = merged_rows // groups
    slots = groups * CAP * rows
    vmem = pl.BlockSpec(memory_space=pltpu.VMEM)
    hbm = pl.BlockSpec(memory_space=pltpu.HBM)
    low, full = jnp.bfloat16, jnp.float32
    return pl.pallas_call(
        encoder_kernel,
        out_shape=jax.ShapeDtypeStruct((next_weight.shape[0], slots), low),
        in_specs=[hbm, hbm, vmem, vmem, hbm],
        out_specs=vmem,
        scratch_shapes=[
            pltpu.VMEM((groups, CAP, rows, model_width), low),
            pltpu.VMEM(next_weight.shape, low),
            pltpu.VMEM((model_width, slots // 2), low),
            pltpu.VMEM(qkv.shape, low),
            pltpu.VMEM(merge_weight.shape, low),
            pltpu.VMEM((heads, row_len, 2 * TILE), low),
            pltpu.VMEM((heads, SPAN, row_len), low),
            pltpu.VMEM((parts, width, sent), full),
            pltpu.VMEM((parts, heads, sent), full),
            pltpu.VMEM((2, width, sent), full),
            pltpu.VMEM((2, heads, sent), full),
            pltpu.VMEM((2, width, sent), low),
            pltpu.VMEM((2, heads, sent), full),
            pltpu.VMEM((2, heads, sent), full),
            pltpu.VMEM((2, heads, sent), full),
            pltpu.VMEM((2, heads, sent), full),
            pltpu.VMEM((WIN, 2 * tokens, width), low),
            pltpu.VMEM((WIN, 2 * tokens, width), low),
            pltpu.VMEM((WIN, 2 * tokens, width), low),
            pltpu.VMEM((2, 2, tokens // 2, model_width), full),
            pltpu.VMEM((2, 2, tokens // 2, model_width), low),
            pltpu.VMEM((2, tokens // 2, model_width), low),
            pltpu.VMEM((2, tokens // 2, model_width), low),
            pltpu.VMEM((2, tokens // 2, model_width), low),
            pltpu.VMEM((2 * tokens, model_width), full),
            pltpu.VMEM((2 * tokens, model_width), full),
            pltpu.VMEM((2, tokens // 2, model_width), low),
            pltpu.VMEM((2, 2, tokens // 2, model_width), full),
            pltpu.VMEM((2, 2, tokens // 2, model_width), full),
            pltpu.VMEM((merged_rows, model_width), low),
            pltpu.VMEM((merged_rows, model_width), low),
            pltpu.SemaphoreType.DMA((3,)),
            pltpu.SemaphoreType.DMA((WIN,)),
            pltpu.SemaphoreType.DMA,
            pltpu.SemaphoreType.DMA((5, 2)),
            pltpu.SemaphoreType.DMA((5, 2)),
            pltpu.SemaphoreType.DMA((5,)),
            pltpu.SemaphoreType.DMA((5,)),
            pltpu.SemaphoreType.DMA((groups,)),
            pltpu.SemaphoreType.DMA((groups,)),
            pltpu.SemaphoreType.DMA((groups,)),
            pltpu.SemaphoreType.DMA((groups,)),
        ],
        compiler_params=pltpu.CompilerParams(
            vmem_limit_bytes=51 << 20, collective_id=0, has_side_effects=True
        ),
        name="encode",
    )(qkv, merge_weight, gain, ids, next_weight)


def body(qkv, segments, links, owners, merge_weight, norm_gain, norm_bias, next_weight):
    row_len = qkv.shape[1]
    model_width = norm_gain.shape[0]
    tp_size = lax.axis_size("tp")
    turned = jnp.swapaxes(qkv, 1, 2)
    group_count = lax.axis_size("grp")
    owner_ids = owners[0, :, 0]
    block_count = owner_ids.shape[0]
    if tp_size == 2 and block_count == group_count:
        gain = jnp.concatenate([norm_gain, norm_bias])[None]
        ids = jnp.concatenate([segments[0], owner_ids, links])[None]
        projected = encode(turned, merge_weight, gain, ids, next_weight.T, group_count)
        return projected.T[None]
    seg_ids = segments[0]
    linked = links[0] > 0
    sent = row_len // 4
    last_flag = jnp.logical_and(seg_ids == seg_ids[row_len - 1], linked)[row_len - sent :]
    first_flag = (seg_ids == seg_ids[0])[:sent]

    def payload(pairs, flag):
        mark = jnp.broadcast_to(flag.astype(jnp.bfloat16)[None, None, :], (2, PACK, sent))
        return jnp.concatenate([pairs, mark], axis=1)

    prev = shifted(payload(turned[1:3, :, row_len - sent :], last_flag), "grp", 1)
    following = shifted(payload(turned[1:3, :, :sent], first_flag), "grp", -1)
    middle = run_attention(False, turned, segments, merge_weight, sent, None)
    partial_sum = run_attention(
        True, turned, segments, merge_weight, sent, (links, prev, following, middle)
    )
    merged_rows = row_len // WIN

    block_rows = merged_rows // block_count
    block_index = jnp.arange(block_count)
    earlier = block_index[:, None] > block_index[None, :]
    slot_rank = jnp.sum(
        jnp.logical_and(owner_ids[:, None] == owner_ids[None, :], earlier).astype(jnp.int32), axis=1
    )
    slots = group_count * CAP * block_rows

    target = (owner_ids * CAP + slot_rank)[:, None] * block_rows
    target = (target + jnp.arange(block_rows)[None, :]).reshape(merged_rows)
    merged = lax.psum(partial_sum, "tp")
    mean = jnp.mean(merged, axis=1, keepdims=True)
    variance = jnp.mean(merged * merged, axis=1, keepdims=True) - mean * mean
    normed = (merged - mean) * lax.rsqrt(variance + EPS) * norm_gain + norm_bias
    normed = normed.astype(jnp.bfloat16)
    placing = (jnp.arange(slots)[:, None] == target[None, :]).astype(jnp.bfloat16)
    packed = jnp.dot(placing, normed, preferred_element_type=jnp.float32).astype(jnp.bfloat16)
    packed = packed.reshape(group_count, CAP * block_rows, model_width)
    routed = lax.all_to_all(packed, "grp", split_axis=0, concat_axis=0, tiled=True)
    routed = routed.reshape(slots, model_width)
    projected = jnp.dot(routed, next_weight, preferred_element_type=jnp.float32)
    return projected.astype(jnp.bfloat16)[None]


def solution(mesh):
    placed = (
        P(None, "grp", "tp"),
        P("grp", None),
        P("grp"),
        P("grp", None, None),
        P(None, "tp", None),
        P(),
        P(),
        P(None, "tp"),
    )
    return jax.shard_map(
        body, mesh=mesh, in_specs=placed, out_specs=P("grp", None, "tp"), check_vma=False
    )
```
